512 devices in a mesh: req: 128 (over y, z, core), tp: 4 (over x).
Axes of the slice: x: 4, y: 4, z: 16, core: 2. Of those that a mesh axis runs over, the one named last changes fastest.
Arguments:
- queries: bfloat16 [32768, 2048], P('req', 'tp'), may hold values from -160 to 160
- key_rows: bfloat16 [32768, 2048], P('req', 'tp'), may hold values from -6 to 6
- value_rows: bfloat16 [32768, 2048], P('req', 'tp'), may hold values from -6 to 6
- lengths: int32 [128, 4], P('req'), may hold values from 1 to 128, 256 in all within a row
- adapter_ids: int32 [128, 4], P('req'), may hold values from 0 to 127, as said below
- adapter_home: int32 [128], replicated, may hold values from 0 to 127, each once
- adapter_down: bfloat16 [128, 2048, 16], P('req', 'tp'), may hold values from -0.125 to 0.125
- adapter_up: bfloat16 [128, 16, 2048], P('req'), may hold values from -4 to 4
- output_weight: bfloat16 [2048, 2048], P('tp'), may hold values from -0.125 to 0.125
Outputs:
- block_output: bfloat16 [32768, 2048], P('req', 'tp')
The draws below stay inside these ranges and needn't reach their ends.
Inputs may be any that keep to these rules, and one draw needn't show every extreme that they name: `adapter_ids`: all prompts together name exactly 16 distinct adapters.
All inputs are finite; a program needn't handle non-finite values.
Results may differ from the reference program's by a relative error of at most 0.0055.
Values may be sent and summed in bfloat16 or wider, within the bound.
A program may use at most 64 MiB of HBM per device.

```python
import math
import jax
import jax.numpy as jnp
import numpy as np
from jax import lax

D = 2048
HD = 128
RANK = 16
TOK_DEV = 256
SEQ_DEV = 4
AW = 2048
TOKENS = 32768
ADAPTERS = 128
USED = 16
N_REQ = 128


def shared_keys(key):
    return jax.random.truncated_normal(jax.random.fold_in(key, 7), -5.0, 5.0, (TOKENS, AW), jnp.float32)


def draw_key_rows(key, part):
    key_basis = shared_keys(key)
    return key_basis.astype(jnp.bfloat16)


def draw_queries(key, part):
    drawn_rows = jax.random.truncated_normal(jax.random.fold_in(key, 11), -5.0, 5.0, (TOKENS, AW), jnp.float32)
    return drawn_rows.astype(jnp.bfloat16)


def draw_adapter_ids(key, part):
    middle = jax.random.permutation(jax.random.fold_in(key, 1), ADAPTERS - 2)[:USED - 2] + 1
    picked = jnp.concatenate([jnp.array([0, ADAPTERS - 1], dtype=jnp.int32), middle.astype(jnp.int32)])
    spread = jax.random.permutation(jax.random.fold_in(key, 2), N_REQ * SEQ_DEV) % USED
    return picked[spread].reshape(N_REQ, SEQ_DEV).astype(jnp.int32)


def level_of(stream_key, dims, split, smallest, largest):
    def one(axis_at, shards_of):
        draws = jax.random.uniform(jax.random.fold_in(jax.random.fold_in(stream_key, 6), axis_at), (shards_of,), jnp.float32, smallest / len(split), largest / len(split))
        return jnp.repeat(jnp.exp(draws), dims[axis_at] // shards_of).reshape((-1,) + (1,) * (len(dims) - axis_at - 1))

    level = one(*split[0])
    for cut in split[1:]:
        level = level * one(*cut)
    return level


def profile(number_of, total, limit, lean):
    weights = [(1 << 20) // math.isqrt(rank ** lean) + 1 for rank in range(2, number_of + 1)]
    surplus, counts = total - limit - (number_of - 1), [1] * (number_of - 1)
    while surplus > 0:
        candidates = [i for i in range(number_of - 1) if counts[i] < limit]
        pool, remaining = sum([weights[i] for i in candidates]), surplus
        for i in candidates:
            more = min(limit - counts[i], max(1, remaining * weights[i] // pool), surplus)
            counts[i] = counts[i] + more
            surplus = surplus - more
    return np.array([limit] + counts)


def ragged(stream_key, number_of, total, bound, lean):
    if number_of == 2:
        one = jax.random.randint(stream_key, (), max(1, total - bound), min(bound, total - 1) + 1)
        return jnp.stack([one, total - one])
    sizes = jnp.asarray(profile(number_of, total, bound, lean), jnp.int32)
    pairs = (number_of - 1) // 2
    giver, sink = sizes[1:1 + 2 * pairs:2], sizes[2:2 + 2 * pairs:2]
    room = jnp.minimum(giver - 1, bound - sink)
    passed = jax.random.randint(jax.random.fold_in(stream_key, 1), (pairs,), 0, 1 << 20) % (room + 1)
    sizes = sizes.at[1:1 + 2 * pairs:2].set(giver - passed).at[2:2 + 2 * pairs:2].set(sink + passed)
    return sizes[jax.random.permutation(jax.random.fold_in(stream_key, 2), number_of)]


def noise(own_key, shape, scale, reach, cuts=(), held_as=jnp.bfloat16):
    loudness = level_of(own_key, shape, cuts, -0.22, 0.18) if cuts else 1.0
    result = jax.random.normal(own_key, shape, jnp.float32) * scale * loudness
    return jnp.minimum(jnp.maximum(result, -reach), reach).astype(held_as)


def setup_inputs(seed: int = 0) -> dict:
    seeds = jax.random.split(jax.random.key(seed), 10)
    return {
        "queries": draw_queries(jax.random.fold_in(seeds[9], 71), 0),
        "key_rows": draw_key_rows(jax.random.fold_in(seeds[9], 71), 0),
        "value_rows": noise(seeds[2], (TOKENS, AW), 1.0, 6.0, ((0, 128), (1, 4))),
        "lengths": jax.vmap(lambda own: ragged(own, SEQ_DEV, TOK_DEV, TOK_DEV // 2, 2))(jax.random.split(seeds[3], N_REQ)).reshape((N_REQ, SEQ_DEV)).astype(jnp.int32),
        "adapter_ids": draw_adapter_ids(jax.random.fold_in(seeds[9], 71), 0),
        "adapter_home": jax.random.permutation(seeds[5], ADAPTERS).astype(jnp.int32),
        "adapter_down": noise(seeds[6], (ADAPTERS, AW, RANK), AW ** -0.5, 0.125, ((0, 128), (1, 4))),
        "adapter_up": noise(seeds[7], (ADAPTERS, RANK, D), 0.25, 4.0, ((0, 128),)),
        "output_weight": noise(seeds[8], (AW, D), AW ** -0.5, 0.125, ((0, 4),)),
    }


def segment_rows(length_row, row_total):
    boundary = jnp.cumsum(length_row)
    position = jnp.arange(row_total, dtype=jnp.int32)
    return lax.optimization_barrier(jnp.sum((position[:, None] >= boundary[None, :]).astype(jnp.int32), axis=1))

def attend(queries, key_rows, value_rows, segment):
    row_total = queries.shape[0]
    head_count = queries.shape[1] // HD
    shaped_q = queries.reshape(row_total, head_count, HD).astype(jnp.float32)
    shaped_k = key_rows.reshape(row_total, head_count, HD).astype(jnp.float32)
    shaped_v = value_rows.reshape(row_total, head_count, HD).astype(jnp.float32)
    scores = jnp.einsum('qhd,khd->hqk', shaped_q, shaped_k, precision=lax.Precision.HIGHEST) * (1.0 / math.sqrt(HD))
    position = jnp.arange(row_total, dtype=jnp.int32)
    allowed = (segment[:, None] == segment[None, :]) & (position[None, :] <= position[:, None])
    masked = jnp.where(allowed[None], scores, -1e+30)
    highest = lax.optimization_barrier(jnp.max(masked, axis=2, keepdims=True))
    exponent = jnp.where(allowed[None], jnp.exp(masked - highest), 0.0)
    weights = (exponent / lax.optimization_barrier(jnp.sum(exponent, axis=2, keepdims=True))).astype(jnp.bfloat16)
    mixed = jnp.einsum('hqk,khd->qhd', weights.astype(jnp.float32), shaped_v, precision=lax.Precision.HIGHEST)
    return mixed.reshape(row_total, head_count * HD).astype(jnp.bfloat16)

def lowrank_delta(rank_rows, onehot, factor_up):
    row_total, prompts = onehot.shape
    rank_size = rank_rows.shape[1]
    spread = (onehot[:, :, None] * rank_rows[:, None, :]).reshape(row_total, prompts * rank_size)
    upper = factor_up.astype(jnp.float32).reshape(prompts * rank_size, factor_up.shape[2])
    return jnp.dot(spread, upper, precision=lax.Precision.HIGHEST)

def reference(queries, key_rows, value_rows, lengths, adapter_ids, adapter_home, adapter_down, adapter_up, output_weight):
    groups = lengths.shape[0]
    width_all = queries.shape[1]
    grouped_q = queries.reshape(groups, TOK_DEV, width_all)
    grouped_k = key_rows.reshape(groups, TOK_DEV, width_all)
    grouped_v = value_rows.reshape(groups, TOK_DEV, width_all)

    def one_group(items):
        group_q, group_k, group_v, length_row, id_row = items
        segment = segment_rows(length_row, TOK_DEV)
        attended = attend(group_q, group_k, group_v, segment)
        base_rows = jnp.dot(attended, output_weight, preferred_element_type=jnp.float32)
        slot_rows = adapter_home[id_row]
        downs = adapter_down[slot_rows]
        uppers = adapter_up[slot_rows]
        per_prompt = jnp.einsum('ta,sar->str', attended.astype(jnp.float32), downs.astype(jnp.float32), precision=lax.Precision.HIGHEST)
        onehot = (segment[:, None] == jnp.arange(SEQ_DEV, dtype=jnp.int32)[None, :]).astype(jnp.float32)
        low_rank = jnp.einsum('ts,str->tr', onehot, per_prompt, precision=lax.Precision.HIGHEST)
        return (base_rows + lowrank_delta(low_rank, onehot, uppers)).astype(jnp.bfloat16)
    outputs = lax.map(one_group, (grouped_q, grouped_k, grouped_v, lengths, adapter_ids))
    return outputs.reshape(groups * TOK_DEV, outputs.shape[2])
```

```python
import math

import jax
import jax.numpy as jnp
from jax import lax
from jax.experimental import pallas as pl
from jax.experimental.pallas import tpu as pltpu
from jax.sharding import PartitionSpec as P

HD = 128
NY, NZ = 4, 16
LINE = NY * NZ
MESH = pl.DeviceIdType.MESH
F32 = jnp.float32
BF16 = jnp.bfloat16


def stage_offsets(stage):
    if stage == 0:
        return (0,)
    far, near = 2 * stage, 2 * stage - 1
    if far == NZ // 2:
        return (far, NZ - near, near)
    return (NZ - far, far, NZ - near, near)


def kernel(
    len_s,
    ids_s,
    home_s,
    q_h,
    k_h,
    v_h,
    dn_h,
    up_h,
    w_h,
    out_ref,
    qv,
    kv,
    vv,
    wv,
    gd,
    gu,
    att,
    part,
    got,
    fwd_part,
    acc,
    slot_send,
    slot_got,
    slot_s,
    sel_send,
    sel_got,
    low_own,
    low_got,
    load_sem,
    g_send,
    z_recv,
    y_recv,
    o_recv,
    x_send,
    x_recv,
    slot_sem,
    sel_sem,
    low_send,
    low_recv,
):
    req = lax.axis_index("req")
    x = lax.axis_index("tp")
    core = lax.rem(req, 2)
    z = lax.rem(lax.div(req, 2), NZ)
    y = lax.div(req, 2 * NZ)
    rows, width = qv.shape
    half = rows // 2
    prompts = ids_s.shape[1]

    def place(y_at, z_at, core_at):
        return (y_at * NZ + z_at) * 2 + core_at

    def shifted(at, by, size):
        return lax.rem(at + (by + size) % size, size)

    def z_peer(by):
        return (place(y, shifted(z, by, NZ), core), x)

    def y_peer(by):
        return (place(shifted(y, by, NY), z, core), x)

    def x_peer(by):
        return (req, shifted(x, by, 4))

    partner = (place(y, z, 1 - core), x)

    def line(y_by, offset):
        return shifted(y, y_by, NY) * NZ + shifted(z, offset, NZ)

    def remote(src, dst, send, recv, device):
        return pltpu.make_async_remote_copy(
            src_ref=src, dst_ref=dst, send_sem=send, recv_sem=recv, device_id=device, device_id_type=MESH
        )

    banks = (gd, gu)
    own_line = line(0, 0)

    barrier = pltpu.get_barrier_semaphore()
    peers = [z_peer(b) for b in (1, -1, 2, -2)] + [y_peer(1), y_peer(-1), partner] + [x_peer(b) for b in (1, 2, 3)]
    for peer in peers:
        pl.semaphore_signal(barrier, inc=1, device_id=peer, device_id_type=MESH)
    columns = pl.ds(pl.multiple_of(x * width, width), width)
    loads = [
        pltpu.make_async_copy(dn_h.at[0], gd.at[own_line], load_sem.at[0]),
        pltpu.make_async_copy(up_h.at[0, :, columns], gu.at[own_line], load_sem.at[1]),
        pltpu.make_async_copy(q_h, qv, load_sem.at[2]),
        pltpu.make_async_copy(k_h, kv, load_sem.at[3]),
        pltpu.make_async_copy(v_h, vv, load_sem.at[4]),
        pltpu.make_async_copy(w_h, wv, load_sem.at[5]),
    ]
    for load in loads:
        load.start()

    lane = lax.broadcasted_iota(jnp.int32, (8, 128), 1)
    slots = jnp.zeros((8, 128), jnp.int32)
    own_slots = []
    for s in range(prompts):
        home = home_s[ids_s[0, s]]
        own_slots.append(home)
        slots = jnp.where(lane == s, home, slots)
    slot_send[...] = slots

    loads[0].wait()
    loads[1].wait()
    pl.semaphore_wait(barrier, len(peers))

    def z_send(p, offset, by):
        j = line(0, offset)
        remote(
            banks[p].at[j], banks[p].at[j], g_send.at[p], z_recv.at[p, (offset - by) % NZ], z_peer(by)
        ).start()

    def y_send(p, offset):
        j = line(0, offset)
        for way, by in ((0, 1), (1, -1)):
            remote(banks[p].at[j], banks[p].at[j], g_send.at[p], y_recv.at[p, way, offset], y_peer(by)).start()

    def own_sends(p):
        for by in (2, -2, 1, -1):
            z_send(p, 0, by)
        y_send(p, 0)

    def z_stage(p, stage):
        for offset in stage_offsets(stage):
            j = line(0, offset)
            remote(banks[p].at[j], banks[p].at[j], g_send.at[p], z_recv.at[p, offset], z_peer(1)).wait_recv()
            distance = min(offset, NZ - offset)
            if distance == 2 * stage and distance < NZ // 2:
                if offset > NZ // 2:
                    z_send(p, offset, 2)
                    z_send(p, offset, 1)
                else:
                    if distance + 2 < NZ // 2:
                        z_send(p, offset, -2)
                    z_send(p, offset, -1)
            y_send(p, offset)

    def y_stage(p, stage):
        for offset in stage_offsets(stage):
            for way, by in ((0, 1), (1, -1)):
                j = line(-by, offset)
                bank = banks[p].at[j]
                remote(bank, bank, g_send.at[p], y_recv.at[p, way, offset], y_peer(by)).wait_recv()
                if offset % 2 == way:
                    remote(bank, bank, g_send.at[p], o_recv.at[p, offset], y_peer(by)).start()

    def o_stage(p, stage):
        for offset in stage_offsets(stage):
            bank = banks[p].at[line(2, offset)]
            remote(bank, bank, g_send.at[p], o_recv.at[p, offset], y_peer(1)).wait_recv()

    starts = []
    edge = jnp.int32(0)
    for s in range(prompts - 1):
        edge = edge + len_s[0, s]
        starts.append(edge)

    def allowed_of(first, count, keys):
        row = lax.broadcasted_iota(jnp.int32, (count, keys), 0) + first
        key = lax.broadcasted_iota(jnp.int32, (count, keys), 1)
        begin = jnp.zeros((count, keys), jnp.int32)
        for start in starts:
            begin = jnp.where(row >= start, start, begin)
        return (key <= row) & (key >= begin)

    def attend(head, first, keys, allowed):
        cols = slice(head * HD, (head + 1) * HD)
        scores = lax.dot_general(
            qv[first : first + half, cols],
            kv[:keys, cols],
            (((1,), (1,)), ((), ())),
            preferred_element_type=F32,
        ) * (1.0 / math.sqrt(HD))
        masked = jnp.where(allowed, scores, -1e30)
        highest = jnp.max(masked, axis=1, keepdims=True)
        exponent = jnp.exp(masked - highest)
        weights = (exponent * (1.0 / jnp.sum(exponent, axis=1, keepdims=True))).astype(BF16)
        mixed = jnp.dot(weights, vv[:keys, cols], preferred_element_type=F32)
        att[first : first + half, cols] = mixed.astype(BF16)

    def project(first, count, by):
        cols = pl.ds(pl.multiple_of(shifted(x, by, 4) * width, width), width)
        return jnp.dot(att[first : first + count, :], wv[:, cols], preferred_element_type=F32)

    top, low = slice(0, half), slice(half, rows)

    def x_copy(slot, src, dst, by):
        return remote(src, dst, x_send.at[slot], x_recv.at[slot], x_peer(by))

    def x_copies():
        return (
            x_copy(0, part.at[0, top], fwd_part.at[top], 1),
            x_copy(1, part.at[0, low], fwd_part.at[low], -1),
            x_copy(2, part.at[1, top], got.at[0, top], 1),
            x_copy(3, part.at[1, low], got.at[0, low], 1),
            x_copy(4, part.at[2, top], got.at[1, top], -1),
            x_copy(5, part.at[2, low], got.at[1, low], -1),
        )

    xc = x_copies()

    own_sends(0)
    own_sends(1)
    slot_copy = remote(slot_send, slot_got, slot_sem.at[0], slot_sem.at[1], partner)
    slot_copy.start()

    for load in loads[2:5]:
        load.wait()
    allowed_top = allowed_of(0, half, half)
    for head in range(width // HD):
        attend(head, 0, half, allowed_top)
    loads[5].wait()
    part[0, top] = project(0, half, 2).astype(BF16)
    xc[0].start()
    allowed_low = allowed_of(half, half, rows)
    for head in range(width // HD):
        attend(head, half, rows, allowed_low)
    part[0, low] = project(half, half, 2).astype(BF16)
    xc[1].start()

    z_stage(0, 1)
    part[1, low] = project(half, half, 1).astype(BF16)
    xc[3].start()
    part[2, top] = project(0, half, -1).astype(BF16)
    xc[4].start()
    y_stage(0, 0)
    z_stage(1, 1)
    y_stage(1, 0)
    z_stage(0, 2)
    y_stage(0, 1)
    xc[0].wait_recv()
    part[1, top] = (project(0, half, 1) + fwd_part[top].astype(F32)).astype(BF16)
    xc[2].start()
    xc[1].wait_recv()
    part[2, low] = (project(half, half, -1) + fwd_part[low].astype(F32)).astype(BF16)
    xc[5].start()
    z_stage(1, 2)
    y_stage(1, 1)
    z_stage(0, 3)
    y_stage(0, 2)
    acc[...] = project(0, rows, 0)
    z_stage(1, 3)
    y_stage(1, 2)
    z_stage(0, 4)
    y_stage(0, 3)
    z_stage(1, 4)
    slot_copy.wait()
    slot_local = pltpu.make_async_copy(slot_got, slot_s, load_sem.at[6])
    slot_local.start()
    for c in (2, 3, 4, 5):
        xc[c].wait_recv()
    acc[...] += got[0].astype(F32) + got[1].astype(F32)
    slot_local.wait()
    y_stage(0, 4)
    for stage in range(5):
        o_stage(0, stage)

    def pick(p, home):
        return jnp.where(lax.rem(home, 2) == core, banks[p][lax.div(home, 2)], 0).astype(BF16)

    def select(p):
        for s in range(prompts):
            sel_send[p, s] = pick(p, slot_s[0, s])
        copy = remote(sel_send.at[p], sel_got.at[p], sel_sem.at[0, p], sel_sem.at[1, p], partner)
        copy.start()
        return copy

    def chosen(p):
        return jnp.concatenate([pick(p, own_slots[s]) + sel_got[p, s] for s in range(prompts)], axis=0)

    sel0 = select(0)
    y_stage(1, 3)
    sel0.wait()
    rank = gd.shape[1]
    spread = lax.dot_general(chosen(0), att[...], (((1,), (1,)), ((), ())), preferred_element_type=F32)
    token = lax.broadcasted_iota(jnp.int32, (rank, rows), 1)
    bounds = [0] + starts + [rows]

    def in_prompt(s):
        return (token >= bounds[s]) & (token < bounds[s + 1])

    mine = jnp.zeros((rank, rows), F32)
    for s in range(prompts):
        mine = mine + jnp.where(in_prompt(s), spread[s * rank : (s + 1) * rank, :], 0.0)
    low_own[...] = mine
    lows = [remote(low_own, low_got.at[i], low_send.at[i], low_recv.at[i], x_peer(i + 1)) for i in range(3)]
    for copy in lows:
        copy.start()
    y_stage(1, 4)
    for stage in range(5):
        o_stage(1, stage)
    sel1 = select(1)
    sel1.wait()
    factor_up = chosen(1).astype(F32)
    for copy in lows:
        copy.wait()
    total = low_own[...] + low_got[0] + low_got[1] + low_got[2]
    spread = jnp.concatenate([jnp.where(in_prompt(s), total, 0.0) for s in range(prompts)], axis=0)
    delta = jnp.dot(spread.T, factor_up, precision=lax.Precision.HIGHEST, preferred_element_type=F32)
    out_ref[...] = (acc[...] + delta).astype(BF16)

    for copy in xc:
        copy.wait_send()
    for p in range(2):
        sent = banks[p].at[pl.ds(0, LINE - 1)]
        remote(sent, sent, g_send.at[p], g_send.at[p], z_peer(1)).wait_send()


def body(queries, key_rows, value_rows, lengths, adapter_ids, adapter_home, adapter_down, adapter_up, output_weight):
    rows, width = queries.shape
    rank = adapter_up.shape[1]
    prompts = lengths.shape[1]
    dma = pltpu.SemaphoreType.DMA
    smem = pl.BlockSpec(memory_space=pltpu.SMEM)
    hbm = pl.BlockSpec(memory_space=pl.ANY)
    return pl.pallas_call(
        kernel,
        out_shape=jax.ShapeDtypeStruct((rows, width), BF16),
        in_specs=[smem] * 3 + [hbm] * 6,
        out_specs=pl.BlockSpec(memory_space=pltpu.VMEM),
        scratch_shapes=[
            pltpu.VMEM((rows, width), BF16),
            pltpu.VMEM((rows, width), BF16),
            pltpu.VMEM((rows, width), BF16),
            pltpu.VMEM(output_weight.shape, BF16),
            pltpu.VMEM((LINE, rank, width), BF16),
            pltpu.VMEM((LINE, rank, width), BF16),
            pltpu.VMEM((rows, width), BF16),
            pltpu.VMEM((3, rows, width), BF16),
            pltpu.VMEM((2, rows, width), BF16),
            pltpu.VMEM((rows, width), BF16),
            pltpu.VMEM((rows, width), F32),
            pltpu.VMEM((8, 128), jnp.int32),
            pltpu.VMEM((8, 128), jnp.int32),
            pltpu.SMEM((8, 128), jnp.int32),
            pltpu.VMEM((2, prompts, rank, width), BF16),
            pltpu.VMEM((2, prompts, rank, width), BF16),
            pltpu.VMEM((rank, rows), F32),
            pltpu.VMEM((3, rank, rows), F32),
            dma((7,)),
            dma((2,)),
            dma((2, NZ)),
            dma((2, 2, NZ)),
            dma((2, NZ)),
            dma((6,)),
            dma((6,)),
            dma((2,)),
            dma((2, 2)),
            dma((3,)),
            dma((3,)),
        ],
        compiler_params=pltpu.CompilerParams(
            collective_id=0, has_side_effects=True, vmem_limit_bytes=48 * 1024 * 1024
        ),
    )(
        lengths,
        adapter_ids,
        adapter_home,
        queries,
        key_rows,
        value_rows,
        jnp.swapaxes(adapter_down, 1, 2),
        adapter_up,
        output_weight,
    )


def solution(mesh):
    return jax.shard_map(
        body,
        mesh=mesh,
        in_specs=(
            P("req", "tp"),
            P("req", "tp"),
            P("req", "tp"),
            P("req", None),
            P("req", None),
            P(),
            P("req", "tp", None),
            P("req", None, None),
            P("tp", None),
        ),
        out_specs=P("req", "tp"),
        check_vma=False,
    )
```

```python
import math

import jax
import jax.numpy as jnp
from jax import lax
from jax.experimental import pallas as pl
from jax.experimental.pallas import tpu as pltpu
from jax.sharding import PartitionSpec as P

HD = 128
NY, NZ = 4, 16
LINE = NY * NZ
MESH = pl.DeviceIdType.MESH
F32 = jnp.float32
BF16 = jnp.bfloat16


def stage_offsets(stage):
    if stage == 0:
        return (0,)
    far, near = 2 * stage, 2 * stage - 1
    if far == NZ // 2:
        return (far, NZ - near, near)
    return (NZ - far, far, NZ - near, near)


def kernel(
    len_s,
    ids_s,
    home_s,
    q_h,
    k_h,
    v_h,
    dn_h,
    up_h,
    w_h,
    out_ref,
    qv,
    kv,
    vv,
    wv,
    gd,
    gu,
    att,
    part,
    got,
    fwd_part,
    acc,
    slot_send,
    slot_got,
    slot_s,
    sel_send,
    sel_got,
    low_own,
    low_got,
    load_sem,
    g_send,
    z_recv,
    y_recv,
    o_recv,
    x_send,
    x_recv,
    slot_sem,
    sel_sem,
    low_send,
    low_recv,
):
    req = lax.axis_index("req")
    x = lax.axis_index("tp")
    core = lax.rem(req, 2)
    z = lax.rem(lax.div(req, 2), NZ)
    y = lax.div(req, 2 * NZ)
    rows, width = qv.shape
    half = rows // 2
    prompts = ids_s.shape[1]

    def place(y_at, z_at, core_at):
        return (y_at * NZ + z_at) * 2 + core_at

    def shifted(at, by, size):
        return lax.rem(at + (by + size) % size, size)

    def z_peer(by):
        return (place(y, shifted(z, by, NZ), core), x)

    def y_peer(by):
        return (place(shifted(y, by, NY), z, core), x)

    def x_peer(by):
        return (req, shifted(x, by, 4))

    partner = (place(y, z, 1 - core), x)

    def line(y_by, offset):
        return shifted(y, y_by, NY) * NZ + shifted(z, offset, NZ)

    def remote(src, dst, send, recv, device):
        return pltpu.make_async_remote_copy(
            src_ref=src, dst_ref=dst, send_sem=send, recv_sem=recv, device_id=device, device_id_type=MESH
        )

    banks = (gd, gu)
    own_line = line(0, 0)

    barrier = pltpu.get_barrier_semaphore()
    peers = [z_peer(b) for b in (1, -1, 2, -2)] + [y_peer(1), y_peer(-1), partner] + [x_peer(b) for b in (1, 2, 3)]
    for peer in peers:
        pl.semaphore_signal(barrier, inc=1, device_id=peer, device_id_type=MESH)
    columns = pl.ds(pl.multiple_of(x * width, width), width)
    loads = [
        pltpu.make_async_copy(dn_h.at[0], gd.at[own_line], load_sem.at[0]),
        pltpu.make_async_copy(up_h.at[0, :, columns], gu.at[own_line], load_sem.at[1]),
        pltpu.make_async_copy(q_h, qv, load_sem.at[2]),
        pltpu.make_async_copy(k_h, kv, load_sem.at[3]),
        pltpu.make_async_copy(v_h, vv, load_sem.at[4]),
        pltpu.make_async_copy(w_h, wv, load_sem.at[5]),
    ]
    for load in loads:
        load.start()

    lane = lax.broadcasted_iota(jnp.int32, (8, 128), 1)
    slots = jnp.zeros((8, 128), jnp.int32)
    own_slots = []
    for s in range(prompts):
        home = home_s[ids_s[0, s]]
        own_slots.append(home)
        slots = jnp.where(lane == s, home, slots)
    slot_send[...] = slots

    loads[0].wait()
    loads[1].wait()
    pl.semaphore_wait(barrier, len(peers))

    def z_send(p, offset, by):
        j = line(0, offset)
        remote(
            banks[p].at[j], banks[p].at[j], g_send.at[p], z_recv.at[p, (offset - by) % NZ], z_peer(by)
        ).start()

    def y_send(p, offset):
        j = line(0, offset)
        for way, by in ((0, 1), (1, -1)):
            remote(banks[p].at[j], banks[p].at[j], g_send.at[p], y_recv.at[p, way, offset], y_peer(by)).start()

    def own_sends(p):
        for by in (2, -2, 1, -1):
            z_send(p, 0, by)
        y_send(p, 0)

    def z_stage(p, stage):
        for offset in stage_offsets(stage):
            j = line(0, offset)
            remote(banks[p].at[j], banks[p].at[j], g_send.at[p], z_recv.at[p, offset], z_peer(1)).wait_recv()
            distance = min(offset, NZ - offset)
            if distance == 2 * stage and distance < NZ // 2:
                if offset > NZ // 2:
                    z_send(p, offset, 2)
                    z_send(p, offset, 1)
                else:
                    if distance + 2 < NZ // 2:
                        z_send(p, offset, -2)
                    z_send(p, offset, -1)
            y_send(p, offset)

    def y_stage(p, stage):
        for offset in stage_offsets(stage):
            for way, by in ((0, 1), (1, -1)):
                j = line(-by, offset)
                bank = banks[p].at[j]
                remote(bank, bank, g_send.at[p], y_recv.at[p, way, offset], y_peer(by)).wait_recv()
                if offset % 2 == way:
                    remote(bank, bank, g_send.at[p], o_recv.at[p, offset], y_peer(by)).start()

    def o_stage(p, stage):
        for offset in stage_offsets(stage):
            bank = banks[p].at[line(2, offset)]
            remote(bank, bank, g_send.at[p], o_recv.at[p, offset], y_peer(1)).wait_recv()

    starts = []
    edge = jnp.int32(0)
    for s in range(prompts - 1):
        edge = edge + len_s[0, s]
        starts.append(edge)

    def allowed_of(first, count, keys):
        row = lax.broadcasted_iota(jnp.int32, (count, keys), 0) + first
        key = lax.broadcasted_iota(jnp.int32, (count, keys), 1)
        begin = jnp.zeros((count, keys), jnp.int32)
        for start in starts:
            begin = jnp.where(row >= start, start, begin)
        return (key <= row) & (key >= begin)

    def attend(head, first, keys, allowed):
        cols = slice(head * HD, (head + 1) * HD)
        scores = lax.dot_general(
            qv[first : first + half, cols],
            kv[:keys, cols],
            (((1,), (1,)), ((), ())),
            preferred_element_type=F32,
        ) * (1.0 / math.sqrt(HD))
        masked = jnp.where(allowed, scores, -1e30)
        highest = jnp.max(masked, axis=1, keepdims=True)
        exponent = jnp.exp(masked - highest)
        weights = (exponent * (1.0 / jnp.sum(exponent, axis=1, keepdims=True))).astype(BF16)
        mixed = jnp.dot(weights, vv[:keys, cols], preferred_element_type=F32)
        att[first : first + half, cols] = mixed.astype(BF16)

    def project(first, count, by):
        cols = pl.ds(pl.multiple_of(shifted(x, by, 4) * width, width), width)
        return jnp.dot(att[first : first + count, :], wv[:, cols], preferred_element_type=F32)

    top, low = slice(0, half), slice(half, rows)

    def x_copy(slot, src, dst, by):
        return remote(src, dst, x_send.at[slot], x_recv.at[slot], x_peer(by))

    def x_copies():
        return (
            x_copy(0, part.at[0, top], fwd_part.at[top], 1),
            x_copy(1, part.at[0, low], fwd_part.at[low], -1),
            x_copy(2, part.at[1, top], got.at[0, top], 1),
            x_copy(3, part.at[1, low], got.at[0, low], 1),
            x_copy(4, part.at[2, top], got.at[1, top], -1),
            x_copy(5, part.at[2, low], got.at[1, low], -1),
        )

    xc = x_copies()

    own_sends(0)
    own_sends(1)
    slot_copy = remote(slot_send, slot_got, slot_sem.at[0], slot_sem.at[1], partner)
    slot_copy.start()

    for load in loads[2:5]:
        load.wait()
    allowed_top = allowed_of(0, half, half)
    for head in range(width // HD):
        attend(head, 0, half, allowed_top)
    loads[5].wait()
    part[0, top] = project(0, half, 2).astype(BF16)
    xc[0].start()
    allowed_low = allowed_of(half, half, rows)
    for head in range(width // HD):
        attend(head, half, rows, allowed_low)
    part[0, low] = project(half, half, 2).astype(BF16)
    xc[1].start()

    z_stage(0, 1)
    part[1, low] = project(half, half, 1).astype(BF16)
    xc[3].start()
    part[2, top] = project(0, half, -1).astype(BF16)
    xc[4].start()
    y_stage(0, 0)
    z_stage(1, 1)
    y_stage(1, 0)
    z_stage(0, 2)
    y_stage(0, 1)
    xc[0].wait_recv()
    part[1, top] = (project(0, half, 1) + fwd_part[top].astype(F32)).astype(BF16)
    xc[2].start()
    xc[1].wait_recv()
    part[2, low] = (project(half, half, -1) + fwd_part[low].astype(F32)).astype(BF16)
    xc[5].start()
    z_stage(1, 2)
    y_stage(1, 1)
    z_stage(0, 3)
    y_stage(0, 2)
    acc[...] = project(0, rows, 0)
    z_stage(1, 3)
    y_stage(1, 2)
    z_stage(0, 4)
    y_stage(0, 3)
    z_stage(1, 4)
    slot_copy.wait()
    slot_local = pltpu.make_async_copy(slot_got, slot_s, load_sem.at[6])
    slot_local.start()
    for c in (2, 3, 4, 5):
        xc[c].wait_recv()
    acc[...] += got[0].astype(F32) + got[1].astype(F32)
    slot_local.wait()
    y_stage(0, 4)
    for stage in range(5):
        o_stage(0, stage)

    def pick(p, home):
        return jnp.where(lax.rem(home, 2) == core, banks[p][lax.div(home, 2)], 0).astype(BF16)

    def select(p):
        for s in range(prompts):
            sel_send[p, s] = pick(p, slot_s[0, s])
        copy = remote(sel_send.at[p], sel_got.at[p], sel_sem.at[0, p], sel_sem.at[1, p], partner)
        copy.start()
        return copy

    def chosen(p):
        return jnp.concatenate([pick(p, own_slots[s]) + sel_got[p, s] for s in range(prompts)], axis=0)

    sel0 = select(0)
    y_stage(1, 3)
    sel0.wait()
    rank = gd.shape[1]
    spread = lax.dot_general(chosen(0), att[...], (((1,), (1,)), ((), ())), preferred_element_type=F32)
    token = lax.broadcasted_iota(jnp.int32, (rank, rows), 1)
    bounds = [0] + starts + [rows]

    def in_prompt(s):
        return (token >= bounds[s]) & (token < bounds[s + 1])

    mine = jnp.zeros((rank, rows), F32)
    for s in range(prompts):
        mine = mine + jnp.where(in_prompt(s), spread[s * rank : (s + 1) * rank, :], 0.0)
    low_own[...] = mine
    lows = [remote(low_own, low_got.at[i], low_send.at[i], low_recv.at[i], x_peer(i + 1)) for i in range(3)]
    for copy in lows:
        copy.start()
    y_stage(1, 4)
    for stage in range(5):
        o_stage(1, stage)
    sel1 = select(1)
    sel1.wait()
    factor_up = chosen(1).astype(F32)
    for copy in lows:
        copy.wait()
    total = low_own[...] + low_got[0] + low_got[1] + low_got[2]
    spread = jnp.concatenate([jnp.where(in_prompt(s), total, 0.0) for s in range(prompts)], axis=0)
    delta = jnp.dot(spread.T, factor_up, precision=lax.Precision.HIGHEST, preferred_element_type=F32)
    out_ref[...] = (acc[...] + delta).astype(BF16)

    for copy in xc:
        copy.wait_send()
    for p in range(2):
        sent = banks[p].at[pl.ds(0, LINE - 1)]
        remote(sent, sent, g_send.at[p], g_send.at[p], z_peer(1)).wait_send()


def body(queries, key_rows, value_rows, lengths, adapter_ids, adapter_home, adapter_down, adapter_up, output_weight):
    rows, width = queries.shape
    rank = adapter_up.shape[1]
    prompts = lengths.shape[1]
    dma = pltpu.SemaphoreType.DMA
    smem = pl.BlockSpec(memory_space=pltpu.SMEM)
    hbm = pl.BlockSpec(memory_space=pl.ANY)
    return pl.pallas_call(
        kernel,
        out_shape=jax.ShapeDtypeStruct((rows, width), BF16),
        in_specs=[smem] * 3 + [hbm] * 6,
        out_specs=pl.BlockSpec(memory_space=pltpu.VMEM),
        scratch_shapes=[
            pltpu.VMEM((rows, width), BF16),
            pltpu.VMEM((rows, width), BF16),
            pltpu.VMEM((rows, width), BF16),
            pltpu.VMEM(output_weight.shape, BF16),
            pltpu.VMEM((LINE, rank, width), BF16),
            pltpu.VMEM((LINE, rank, width), BF16),
            pltpu.VMEM((rows, width), BF16),
            pltpu.VMEM((3, rows, width), BF16),
            pltpu.VMEM((2, rows, width), BF16),
            pltpu.VMEM((rows, width), BF16),
            pltpu.VMEM((rows, width), F32),
            pltpu.VMEM((8, 128), jnp.int32),
            pltpu.VMEM((8, 128), jnp.int32),
            pltpu.SMEM((8, 128), jnp.int32),
            pltpu.VMEM((2, prompts, rank, width), BF16),
            pltpu.VMEM((2, prompts, rank, width), BF16),
            pltpu.VMEM((rank, rows), F32),
            pltpu.VMEM((3, rank, rows), F32),
            dma((7,)),
            dma((2,)),
            dma((2, NZ)),
            dma((2, 2, NZ)),
            dma((2, NZ)),
            dma((6,)),
            dma((6,)),
            dma((2,)),
            dma((2, 2)),
            dma((3,)),
            dma((3,)),
        ],
        compiler_params=pltpu.CompilerParams(
            collective_id=0, has_side_effects=True, vmem_limit_bytes=67_043_328
        ),
    )(
        lengths,
        adapter_ids,
        adapter_home,
        queries,
        key_rows,
        value_rows,
        jnp.swapaxes(adapter_down, 1, 2),
        adapter_up,
        output_weight,
    )


def solution(mesh):
    return jax.shard_map(
        body,
        mesh=mesh,
        in_specs=(
            P("req", "tp"),
            P("req", "tp"),
            P("req", "tp"),
            P("req", None),
            P("req", None),
            P(),
            P("req", "tp", None),
            P("req", None, None),
            P("tp", None),
        ),
        out_specs=P("req", "tp"),
        check_vma=False,
    )
```

```python
import math

import jax
import jax.numpy as jnp
from jax import lax
from jax.experimental import pallas as pl
from jax.experimental.pallas import tpu as pltpu
from jax.sharding import PartitionSpec as P

HD = 128
NY, NZ, NX = 4, 16, 4
LINE = NY * NZ
MESH = pl.DeviceIdType.MESH
F32 = jnp.float32
BF16 = jnp.bfloat16

DOWN_TREE = {0: (4, 2, 1), 2: (3,), 4: (8, 6, 5), 6: (7,)}
UP_TREE = {0: (2, 1), 2: (4, 3), 4: (6, 5), 6: (8, 7)}


def offsets_at(distance):
    return (distance,) if distance in (0, NZ // 2) else (NZ - distance, distance)


def kernel(
    len_h,
    ids_h,
    home_h,
    q_h,
    k_h,
    v_h,
    dn_h,
    up_h,
    w_h,
    out_ref,
    len_s,
    ids_s,
    home_s,
    qv,
    kv,
    vv,
    wv,
    gd,
    gu,
    att,
    att_other,
    part,
    got,
    fwd_part,
    acc,
    note_all,
    note_s,
    pre_send,
    pre_got,
    up_send,
    up_got,
    low_send_buf,
    low_got,
    load_sem,
    d_send,
    u_send,
    zd_recv,
    zu_recv,
    y_recv,
    o_recv,
    x_send,
    x_recv,
    note_send,
    note_recv,
    att_sem,
    pre_sem,
    up_sem_send,
    up_sem_recv,
    low_send,
    low_recv,
):
    req = lax.axis_index("req")
    x = lax.axis_index("tp")
    core = lax.rem(req, 2)
    z = lax.rem(lax.div(req, 2), NZ)
    y = lax.div(req, 2 * NZ)
    rows, width = qv.shape
    half = rows // 2
    prompts = ids_s.shape[1]
    rank = gd.shape[1]

    def place(y_at, z_at, core_at):
        return (y_at * NZ + z_at) * 2 + core_at

    def shifted(at, by, size):
        return lax.rem(at + by % size, size)

    def z_peer(by):
        return (place(y, shifted(z, by, NZ), core), x)

    def y_peer(by, other=0):
        return (place(shifted(y, by, NY), z, 1 - core if other else core), x)

    def x_peer(by, other=0):
        return (place(y, z, 1 - core if other else core), shifted(x, by, NX))

    partner = y_peer(0, 1)

    def line(y_by, offset):
        return shifted(y, y_by, NY) * NZ + shifted(z, offset, NZ)

    def remote(src, dst, send, recv, device):
        return pltpu.make_async_remote_copy(
            src_ref=src, dst_ref=dst, send_sem=send, recv_sem=recv, device_id=device, device_id_type=MESH
        )

    plane = [(by, other) for by in range(NY) for other in range(2) if (by, other) != (0, 0)]

    columns = pl.ds(pl.multiple_of(x * width, width), width)
    loads = [
        pltpu.make_async_copy(dn_h.at[0], gd.at[line(0, 0)], load_sem.at[0]),
        pltpu.make_async_copy(up_h.at[0, :, columns], gu.at[z], load_sem.at[1]),
        pltpu.make_async_copy(len_h, len_s, load_sem.at[2]),
        pltpu.make_async_copy(ids_h, ids_s, load_sem.at[3]),
        pltpu.make_async_copy(home_h, home_s, load_sem.at[4]),
        pltpu.make_async_copy(q_h, qv, load_sem.at[5]),
        pltpu.make_async_copy(k_h, kv, load_sem.at[6]),
        pltpu.make_async_copy(v_h, vv, load_sem.at[7]),
        pltpu.make_async_copy(w_h, wv, load_sem.at[8]),
    ]
    for load in loads:
        load.start()
    barrier = pltpu.get_barrier_semaphore()
    peers = [z_peer(b) for b in (4, -4, 2, -2, 1, -1)] + [y_peer(b, o) for b, o in plane]
    peers += [x_peer(b, o) for b in range(1, NX) for o in range(2)]
    for peer in peers:
        pl.semaphore_signal(barrier, inc=1, device_id=peer, device_id_type=MESH)
    loads[0].wait()
    pl.semaphore_wait(barrier, len(peers))

    def z_bank(p, offset):
        return gu.at[shifted(z, offset, NZ)] if p else gd.at[line(0, offset)]

    z_recv = (zd_recv, zu_recv)
    z_send_sem = (d_send, u_send)
    trees = (DOWN_TREE, UP_TREE)

    def z_pass(p, offset):
        distance = min(offset, NZ - offset)
        for target in trees[p].get(distance, ()):
            for sign in (1, -1):
                if target == NZ // 2 and sign < 0:
                    continue
                if distance and (offset > NZ // 2) != (sign > 0):
                    continue
                by = sign * (target - distance)
                bank = z_bank(p, offset)
                remote(bank, bank, z_send_sem[p], z_recv[p].at[(offset - by) % NZ], z_peer(by)).start()

    def y_pass(offset):
        bank = gd.at[line(0, offset)]
        for way, by in ((0, 1), (1, -1)):
            remote(bank, bank, d_send, y_recv.at[way, offset], y_peer(by)).start()

    def z_take(p, *distances):
        for distance in distances:
            for offset in offsets_at(distance):
                bank = z_bank(p, offset)
                remote(bank, bank, z_send_sem[p], z_recv[p].at[offset], z_peer(1)).wait_recv()
                z_pass(p, offset)
                if p == 0:
                    y_pass(offset)

    def y_take(*distances):
        for distance in distances:
            for offset in offsets_at(distance):
                for way, by in ((0, 1), (1, -1)):
                    bank = gd.at[line(-by, offset)]
                    remote(bank, bank, d_send, y_recv.at[way, offset], y_peer(by)).wait_recv()
                    if (distance % 2 if distance < NZ // 2 else offset // NZ) == way:
                        remote(bank, bank, d_send, o_recv.at[offset], y_peer(by)).start()

    def o_take(*distances):
        for distance in distances:
            for offset in offsets_at(distance):
                bank = gd.at[line(2, offset)]
                remote(bank, bank, d_send, o_recv.at[offset], y_peer(1)).wait_recv()

    z_pass(0, 0)
    y_pass(0)
    loads[1].wait()
    z_pass(1, 0)

    for load in loads[2:5]:
        load.wait()
    starts = []
    edge = jnp.int32(0)
    for s in range(prompts - 1):
        edge = edge + len_s[0, s]
        starts.append(edge)
    homes = [home_s[ids_s[0, s]] for s in range(prompts)]
    lane = lax.broadcasted_iota(jnp.int32, (8, 128), 1)
    note = jnp.zeros((8, 128), jnp.int32)
    for i, value in enumerate(homes + starts):
        note = jnp.where(lane == i, value, note)
    note_all[0] = note
    notes = []
    for i, (by, other) in enumerate(plane):
        spot = 2 * ((NY - by) % NY) + other
        notes.append(remote(note_all.at[0], note_all.at[spot], note_send.at[i], note_recv.at[i], y_peer(by, other)))
    for copy in notes:
        copy.start()

    def allowed_of(first, count, keys):
        row = lax.broadcasted_iota(jnp.int32, (count, keys), 0) + first
        key = lax.broadcasted_iota(jnp.int32, (count, keys), 1)
        begin = jnp.zeros((count, keys), jnp.int32)
        for start in starts:
            begin = jnp.where(row >= start, start, begin)
        return (key <= row) & (key >= begin)

    def attend(first, keys):
        allowed = allowed_of(first, half, keys)
        for head in range(width // HD):
            cols = slice(head * HD, (head + 1) * HD)
            scores = lax.dot_general(
                qv[first : first + half, cols],
                kv[:keys, cols],
                (((1,), (1,)), ((), ())),
                preferred_element_type=F32,
            ) * (1.0 / math.sqrt(HD))
            masked = jnp.where(allowed, scores, -1e30)
            highest = jnp.max(masked, axis=1, keepdims=True)
            exponent = jnp.exp(masked - highest)
            weights = (exponent * (1.0 / jnp.sum(exponent, axis=1, keepdims=True))).astype(BF16)
            mixed = jnp.dot(weights, vv[:keys, cols], preferred_element_type=F32)
            att[first : first + half, cols] = mixed.astype(BF16)

    def project(first, count, by):
        cols = pl.ds(pl.multiple_of(shifted(x, by, NX) * width, width), width)
        return jnp.dot(att[first : first + count, :], wv[:, cols], preferred_element_type=F32)

    top, low = slice(0, half), slice(half, rows)

    def x_copy(slot, src, dst, by):
        return remote(src, dst, x_send.at[slot], x_recv.at[slot], x_peer(by))

    xc = (
        x_copy(0, part.at[0, top], fwd_part.at[top], 1),
        x_copy(1, part.at[0, low], fwd_part.at[low], -1),
        x_copy(2, part.at[1, top], got.at[0, top], 1),
        x_copy(3, part.at[1, low], got.at[0, low], 1),
        x_copy(4, part.at[2, top], got.at[1, top], -1),
        x_copy(5, part.at[2, low], got.at[1, low], -1),
    )

    for load in loads[5:8]:
        load.wait()
    attend(0, half)
    loads[8].wait()
    part[0, top] = project(0, half, 2).astype(BF16)
    xc[0].start()
    z_take(0, 1, 2)
    attend(half, rows)
    part[0, low] = project(half, half, 2).astype(BF16)
    xc[1].start()
    att_copy = remote(att, att_other, att_sem.at[0], att_sem.at[1], partner)
    att_copy.start()
    part[1, low] = project(half, half, 1).astype(BF16)
    xc[3].start()
    part[2, top] = project(0, half, -1).astype(BF16)
    xc[4].start()
    z_take(0, 4)
    z_take(1, 2, 1)
    z_take(0, 3)
    y_take(0, 1, 2)
    part[1, top] = project(0, half, 1).astype(BF16)
    part[2, low] = project(half, half, -1).astype(BF16)
    acc[...] = project(0, rows, 0)
    for copy in notes:
        copy.wait()
    notes_local = pltpu.make_async_copy(note_all, note_s, load_sem.at[9])
    notes_local.start()
    xc[0].wait_recv()
    part[1, top] = (part[1, top].astype(F32) + fwd_part[top].astype(F32)).astype(BF16)
    xc[2].start()
    xc[1].wait_recv()
    part[2, low] = (part[2, low].astype(F32) + fwd_part[low].astype(F32)).astype(BF16)
    xc[5].start()
    z_take(1, 4, 3)
    z_take(0, 5, 6)
    y_take(3, 4)
    z_take(0, 8, 7)
    z_take(1, 6, 5)
    y_take(5, 6)
    notes_local.wait()
    z_take(1, 8, 7)

    def pick_up(spot, s):
        home = note_s[spot, 0, s]
        mine = (lax.rem(home, 2) == core) & (lax.div(home, 2 * NZ) == y)
        return jnp.where(mine, gu[lax.rem(lax.div(home, 2), NZ)], 0).astype(BF16)

    for by in range(NY):
        for s in range(prompts):
            pre_send[by, s] = pick_up(2 * by + 1, s)
    pre = remote(pre_send, pre_got, pre_sem.at[0], pre_sem.at[1], partner)
    pre.start()
    for by in range(NY):
        for s in range(prompts):
            up_send[by, s] = pick_up(2 * by, s)
    y_take(8, 7)
    pre.wait()
    ups = []
    for by in (2, 1, 3):
        up_send[by] = up_send[by] + pre_got[by]
        ups.append(remote(up_send.at[by], up_got.at[by - 1], up_sem_send.at[by - 1], up_sem_recv.at[by - 1], y_peer(by)))
        ups[-1].start()
    for c in (2, 3, 4, 5):
        xc[c].wait_recv()
    acc[...] += got[0].astype(F32) + got[1].astype(F32)
    att_copy.wait()
    o_take(0, 1, 2, 3, 4, 5, 6, 8, 7)

    token = lax.broadcasted_iota(jnp.int32, (rank, rows), 1)

    def in_prompt(s, begins):
        inside = token >= begins[s - 1] if s else token >= 0
        return inside & (token < begins[s]) if s < prompts - 1 else inside

    def low_rank(spot, rows_ref):
        factors = []
        for s in range(prompts):
            home = note_s[spot, 0, s]
            factors.append(jnp.where(lax.rem(home, 2) == core, gd[lax.div(home, 2)], 0).astype(BF16))
        begins = [note_s[spot, 0, prompts + s] for s in range(prompts - 1)]
        every = lax.dot_general(
            jnp.concatenate(factors, axis=0), rows_ref[...], (((1,), (1,)), ((), ())), preferred_element_type=F32
        )
        total = jnp.zeros((rank, rows), F32)
        for s in range(prompts):
            total = total + jnp.where(in_prompt(s, begins), every[s * rank : (s + 1) * rank, :], 0.0)
        return total

    low_send_buf[0] = low_rank(0, att)
    lows = []

    def low_copy(which, spot, device):
        copy = remote(low_send_buf.at[which], low_got.at[spot], low_send.at[spot], low_recv.at[spot], device)
        copy.start()
        lows.append(copy)

    for by in (2, 1, 3):
        low_copy(0, by - 1, x_peer(by))
    low_send_buf[1] = low_rank(1, att_other)
    for by in (2, 1, 3, 0):
        low_copy(1, by + 3, x_peer(by, 1))

    factor_up = up_send[0] + pre_got[0]
    for copy in ups:
        copy.wait()
    factor_up = (factor_up + up_got[0]) + (up_got[1] + up_got[2])
    factor_up = factor_up.reshape(prompts * rank, width)
    for copy in lows:
        copy.wait()
    total = low_send_buf[0]
    for spot in range(7):
        total = total + low_got[spot]
    spread = jnp.concatenate([jnp.where(in_prompt(s, starts), total, 0.0) for s in range(prompts)], axis=0).T
    high = spread.astype(BF16)
    rest = (spread - high.astype(F32)).astype(BF16)
    delta = jnp.dot(high, factor_up, preferred_element_type=F32) + jnp.dot(
        rest, factor_up, preferred_element_type=F32
    )
    out_ref[...] = (acc[...] + delta).astype(BF16)

    for copy in xc:
        copy.wait_send()
    sent = gd.at[pl.ds(0, LINE - 1)]
    remote(sent, sent, d_send, d_send, z_peer(1)).wait_send()
    sent = gu.at[pl.ds(0, NZ - 1)]
    remote(sent, sent, u_send, u_send, z_peer(1)).wait_send()


def body(queries, key_rows, value_rows, lengths, adapter_ids, adapter_home, adapter_down, adapter_up, output_weight):
    rows, width = queries.shape
    rank = adapter_up.shape[1]
    prompts = lengths.shape[1]
    dma = pltpu.SemaphoreType.DMA
    hbm = pl.BlockSpec(memory_space=pltpu.HBM)
    block = pltpu.VMEM((rows, width), BF16)
    return pl.pallas_call(
        kernel,
        out_shape=jax.ShapeDtypeStruct((rows, width), BF16),
        in_specs=[hbm] * 9,
        out_specs=pl.BlockSpec(memory_space=pltpu.VMEM),
        scratch_shapes=[
            pltpu.SMEM(lengths.shape, jnp.int32),
            pltpu.SMEM(adapter_ids.shape, jnp.int32),
            pltpu.SMEM(adapter_home.shape, jnp.int32),
            block,
            block,
            block,
            pltpu.VMEM(output_weight.shape, BF16),
            pltpu.VMEM((LINE, rank, width), BF16),
            pltpu.VMEM((NZ, rank, width), BF16),
            block,
            block,
            pltpu.VMEM((3, rows, width), BF16),
            pltpu.VMEM((2, rows, width), BF16),
            block,
            pltpu.VMEM((rows, width), F32),
            pltpu.VMEM((2 * NY, 8, 128), jnp.int32),
            pltpu.SMEM((2 * NY, 8, 128), jnp.int32),
            pltpu.VMEM((NY, prompts, rank, width), BF16),
            pltpu.VMEM((NY, prompts, rank, width), BF16),
            pltpu.VMEM((NY, prompts, rank, width), BF16),
            pltpu.VMEM((NY - 1, prompts, rank, width), BF16),
            pltpu.VMEM((2, rank, rows), F32),
            pltpu.VMEM((7, rank, rows), F32),
            dma((10,)),
            dma,
            dma,
            dma((NZ,)),
            dma((NZ,)),
            dma((2, NZ)),
            dma((NZ,)),
            dma((6,)),
            dma((6,)),
            dma((7,)),
            dma((7,)),
            dma((2,)),
            dma((2,)),
            dma((3,)),
            dma((3,)),
            dma((7,)),
            dma((7,)),
        ],
        compiler_params=pltpu.CompilerParams(
            collective_id=0, has_side_effects=True, vmem_limit_bytes=VMEM_LIMIT
        ),
    )(
        lengths,
        adapter_ids,
        adapter_home,
        queries,
        key_rows,
        value_rows,
        jnp.swapaxes(adapter_down, 1, 2),
        adapter_up,
        output_weight,
    )


VMEM_LIMIT = 67_043_328


def solution(mesh):
    return jax.shard_map(
        body,
        mesh=mesh,
        in_specs=(
            P("req", "tp"),
            P("req", "tp"),
            P("req", "tp"),
            P("req", None),
            P("req", None),
            P(),
            P("req", "tp", None),
            P("req", None, None),
            P("tp", None),
        ),
        out_specs=P("req", "tp"),
        check_vma=False,
    )
```

```python
import math

import jax
import jax.numpy as jnp
from jax import lax
from jax.experimental import pallas as pl
from jax.experimental.pallas import tpu as pltpu
from jax.sharding import PartitionSpec as P

HD = 128
NY, NZ, NX = 4, 16, 4
LINE = NY * NZ
MESH = pl.DeviceIdType.MESH
F32 = jnp.float32
BF16 = jnp.bfloat16

TREE = {0: (4, 2, 1), 2: (3,), 4: (8, 6, 5), 6: (7,)}


def offsets_at(distance):
    return (distance,) if distance in (0, NZ // 2) else (NZ - distance, distance)


def kernel(
    len_h,
    ids_h,
    home_h,
    q_h,
    k_h,
    v_h,
    dn_h,
    up_h,
    w_h,
    out_ref,
    len_s,
    ids_s,
    home_s,
    qv,
    kv,
    vv,
    wv,
    gd,
    gu,
    att,
    att_other,
    part,
    got,
    fwd_part,
    acc,
    note_all,
    note_s,
    up_send,
    up_got,
    low_send_buf,
    low_got,
    load_sem,
    d_send,
    u_send,
    zd_recv,
    zu_recv,
    y_recv,
    o_recv,
    x_send,
    x_recv,
    note_send,
    note_recv,
    att_sem,
    piece_send,
    piece_recv,
    up_sem_send,
    up_sem_recv,
    low_send,
    low_recv,
):
    req = lax.axis_index("req")
    x = lax.axis_index("tp")
    core = lax.rem(req, 2)
    z = lax.rem(lax.div(req, 2), NZ)
    y = lax.div(req, 2 * NZ)
    rows, width = qv.shape
    half = rows // 2
    prompts = ids_s.shape[1]
    rank = gd.shape[1]

    def place(y_at, z_at, core_at):
        return (y_at * NZ + z_at) * 2 + core_at

    def shifted(at, by, size):
        return lax.rem(at + by % size, size)

    def z_peer(by):
        return (place(y, shifted(z, by, NZ), core), x)

    def y_peer(by, other=0):
        return (place(shifted(y, by, NY), z, 1 - core if other else core), x)

    def x_peer(by, other=0):
        return (place(y, z, 1 - core if other else core), shifted(x, by, NX))

    partner = y_peer(0, 1)

    def line(y_by, offset):
        return shifted(y, y_by, NY) * NZ + shifted(z, offset, NZ)

    def remote(src, dst, send, recv, device):
        return pltpu.make_async_remote_copy(
            src_ref=src, dst_ref=dst, send_sem=send, recv_sem=recv, device_id=device, device_id_type=MESH
        )

    plane = [(by, other) for by in range(NY) for other in range(2) if (by, other) != (0, 0)]

    seat = 2 * y + core
    tile = width // NY

    def piece_of(by, other):
        first = pl.multiple_of((1 - core if other else core) * (rank // 2), rank // 2)
        column = pl.multiple_of(x * width + shifted(y, by, NY) * tile, tile)
        return up_h.at[0, pl.ds(first, rank // 2), pl.ds(column, tile)]

    loads = [
        pltpu.make_async_copy(dn_h.at[0], gd.at[line(0, 0)], load_sem.at[0]),
        pltpu.make_async_copy(piece_of(0, 0), gu.at[z, seat], load_sem.at[1]),
        pltpu.make_async_copy(len_h, len_s, load_sem.at[2]),
        pltpu.make_async_copy(ids_h, ids_s, load_sem.at[3]),
        pltpu.make_async_copy(home_h, home_s, load_sem.at[4]),
        pltpu.make_async_copy(q_h, qv, load_sem.at[5]),
        pltpu.make_async_copy(k_h, kv, load_sem.at[6]),
        pltpu.make_async_copy(v_h, vv, load_sem.at[7]),
        pltpu.make_async_copy(w_h, wv, load_sem.at[8]),
    ]
    for load in loads:
        load.start()
    barrier = pltpu.get_barrier_semaphore()
    peers = [z_peer(b) for b in (4, -4, 2, -2, 1, -1)] + [y_peer(b, o) for b, o in plane]
    peers += [x_peer(b, o) for b in range(1, NX) for o in range(2)]
    for peer in peers:
        pl.semaphore_signal(barrier, inc=1, device_id=peer, device_id_type=MESH)
    loads[0].wait()
    pl.semaphore_wait(barrier, len(peers))

    def z_bank(p, offset):
        return gu.at[shifted(z, offset, NZ)] if p else gd.at[line(0, offset)]

    z_recv = (zd_recv, zu_recv)
    z_send_sem = (d_send, u_send)

    def z_pass(p, offset):
        distance = min(offset, NZ - offset)
        for target in TREE.get(distance, ()):
            for sign in (1, -1):
                if target == NZ // 2 and sign < 0:
                    continue
                if distance and (offset > NZ // 2) != (sign > 0):
                    continue
                by = sign * (target - distance)
                bank = z_bank(p, offset)
                remote(bank, bank, z_send_sem[p], z_recv[p].at[(offset - by) % NZ], z_peer(by)).start()

    def y_pass(offset):
        bank = gd.at[line(0, offset)]
        for way, by in ((0, 1), (1, -1)):
            remote(bank, bank, d_send, y_recv.at[way, offset], y_peer(by)).start()

    def z_take(p, *distances):
        for distance in distances:
            for offset in offsets_at(distance):
                bank = z_bank(p, offset)
                remote(bank, bank, z_send_sem[p], z_recv[p].at[offset], z_peer(1)).wait_recv()
                z_pass(p, offset)
                if p == 0:
                    y_pass(offset)

    def y_take(*distances):
        for distance in distances:
            for offset in offsets_at(distance):
                for way, by in ((0, 1), (1, -1)):
                    bank = gd.at[line(-by, offset)]
                    remote(bank, bank, d_send, y_recv.at[way, offset], y_peer(by)).wait_recv()
                    if (distance % 2 if distance < NZ // 2 else offset // NZ) == way:
                        remote(bank, bank, d_send, o_recv.at[offset], y_peer(by)).start()

    def o_take(*distances):
        for distance in distances:
            for offset in offsets_at(distance):
                bank = gd.at[line(2, offset)]
                remote(bank, bank, d_send, o_recv.at[offset], y_peer(1)).wait_recv()

    z_pass(0, 0)
    y_pass(0)
    pieces = [
        remote(piece_of(by, other), gu.at[z, seat], piece_send.at[i], piece_recv.at[i], y_peer(by, other))
        for i, (by, other) in enumerate(plane)
    ]
    for copy in pieces:
        copy.start()

    for load in loads[2:5]:
        load.wait()
    starts = []
    edge = jnp.int32(0)
    for s in range(prompts - 1):
        edge = edge + len_s[0, s]
        starts.append(edge)
    homes = [home_s[ids_s[0, s]] for s in range(prompts)]
    lane = lax.broadcasted_iota(jnp.int32, (8, 128), 1)
    note = jnp.zeros((8, 128), jnp.int32)
    for i, value in enumerate(homes + starts):
        note = jnp.where(lane == i, value, note)
    note_all[0] = note
    notes = []
    for i, (by, other) in enumerate(plane):
        spot = 2 * ((NY - by) % NY) + other
        notes.append(remote(note_all.at[0], note_all.at[spot], note_send.at[i], note_recv.at[i], y_peer(by, other)))
    for copy in notes:
        copy.start()

    def allowed_of(first, count, keys):
        row = lax.broadcasted_iota(jnp.int32, (count, keys), 0) + first
        key = lax.broadcasted_iota(jnp.int32, (count, keys), 1)
        begin = jnp.zeros((count, keys), jnp.int32)
        for start in starts:
            begin = jnp.where(row >= start, start, begin)
        return (key <= row) & (key >= begin)

    def attend(first, keys):
        allowed = allowed_of(first, half, keys)
        for head in range(width // HD):
            cols = slice(head * HD, (head + 1) * HD)
            scores = lax.dot_general(
                qv[first : first + half, cols],
                kv[:keys, cols],
                (((1,), (1,)), ((), ())),
                preferred_element_type=F32,
            ) * (1.0 / math.sqrt(HD))
            masked = jnp.where(allowed, scores, -1e30)
            highest = jnp.max(masked, axis=1, keepdims=True)
            exponent = jnp.exp(masked - highest)
            weights = (exponent * (1.0 / jnp.sum(exponent, axis=1, keepdims=True))).astype(BF16)
            mixed = jnp.dot(weights, vv[:keys, cols], preferred_element_type=F32)
            att[first : first + half, cols] = mixed.astype(BF16)

    def project(first, count, by):
        cols = pl.ds(pl.multiple_of(shifted(x, by, NX) * width, width), width)
        return jnp.dot(att[first : first + count, :], wv[:, cols], preferred_element_type=F32)

    top, low = slice(0, half), slice(half, rows)

    def x_copy(slot, src, dst, by):
        return remote(src, dst, x_send.at[slot], x_recv.at[slot], x_peer(by))

    xc = (
        x_copy(0, part.at[0, top], fwd_part.at[top], 1),
        x_copy(1, part.at[0, low], fwd_part.at[low], -1),
        x_copy(2, part.at[1, top], got.at[0, top], 1),
        x_copy(3, part.at[1, low], got.at[0, low], 1),
        x_copy(4, part.at[2, top], got.at[1, top], -1),
        x_copy(5, part.at[2, low], got.at[1, low], -1),
    )

    for load in loads[5:8]:
        load.wait()
    attend(0, half)
    loads[8].wait()
    part[0, top] = project(0, half, 2).astype(BF16)
    xc[0].start()
    z_take(0, 1, 2)
    loads[1].wait()
    for copy in pieces:
        copy.wait()
    z_pass(1, 0)
    attend(half, rows)
    part[0, low] = project(half, half, 2).astype(BF16)
    xc[1].start()
    att_copy = remote(att, att_other, att_sem.at[0], att_sem.at[1], partner)
    att_copy.start()
    part[1, low] = project(half, half, 1).astype(BF16)
    xc[3].start()
    part[2, top] = project(0, half, -1).astype(BF16)
    xc[4].start()
    z_take(0, 4, 3)
    y_take(0, 1, 2)
    part[1, top] = project(0, half, 1).astype(BF16)
    part[2, low] = project(half, half, -1).astype(BF16)
    acc[...] = project(0, rows, 0)
    for copy in notes:
        copy.wait()
    notes_local = pltpu.make_async_copy(note_all, note_s, load_sem.at[9])
    notes_local.start()
    xc[0].wait_recv()
    part[1, top] = (part[1, top].astype(F32) + fwd_part[top].astype(F32)).astype(BF16)
    xc[2].start()
    xc[1].wait_recv()
    part[2, low] = (part[2, low].astype(F32) + fwd_part[low].astype(F32)).astype(BF16)
    xc[5].start()
    z_take(1, 1, 2, 4)
    z_take(0, 5, 6)
    y_take(3, 4)
    z_take(0, 8, 7)
    z_take(1, 3)
    notes_local.wait()
    y_take(5, 6, 8, 7)
    z_take(1, 5, 6, 8, 7)

    def pick_up(spot, s):
        home = note_s[spot, 0, s]
        return gu[lax.rem(lax.div(home, 2), NZ), 2 * lax.div(home, 2 * NZ) + lax.rem(home, 2)]

    ups = []
    for i, (by, other) in enumerate(plane):
        for s in range(prompts):
            up_send[i, s] = pick_up(2 * by + other, s)
        ups.append(remote(up_send.at[i], up_got.at[seat], up_sem_send.at[i], up_sem_recv.at[i], y_peer(by, other)))
        ups[-1].start()
    for s in range(prompts):
        up_got[seat, s] = pick_up(0, s)
    for c in (2, 3, 4, 5):
        xc[c].wait_recv()
    acc[...] += got[0].astype(F32) + got[1].astype(F32)
    att_copy.wait()
    o_take(0, 1, 2, 3, 4, 5, 6, 8, 7)

    token = lax.broadcasted_iota(jnp.int32, (rank, rows), 1)

    def in_prompt(s, begins):
        inside = token >= begins[s - 1] if s else token >= 0
        return inside & (token < begins[s]) if s < prompts - 1 else inside

    def low_rank(spot, rows_ref):
        factors = []
        for s in range(prompts):
            home = note_s[spot, 0, s]
            factors.append(jnp.where(lax.rem(home, 2) == core, gd[lax.div(home, 2)], 0).astype(BF16))
        begins = [note_s[spot, 0, prompts + s] for s in range(prompts - 1)]
        every = lax.dot_general(
            jnp.concatenate(factors, axis=0), rows_ref[...], (((1,), (1,)), ((), ())), preferred_element_type=F32
        )
        total = jnp.zeros((rank, rows), F32)
        for s in range(prompts):
            total = total + jnp.where(in_prompt(s, begins), every[s * rank : (s + 1) * rank, :], 0.0)
        return total

    low_send_buf[0] = low_rank(0, att)
    lows = []

    def low_copy(which, spot, device):
        copy = remote(low_send_buf.at[which], low_got.at[spot], low_send.at[spot], low_recv.at[spot], device)
        copy.start()
        lows.append(copy)

    for by in (2, 1, 3):
        low_copy(0, by - 1, x_peer(by))
    low_send_buf[1] = low_rank(1, att_other)
    for by in (2, 1, 3, 0):
        low_copy(1, by + 3, x_peer(by, 1))

    for copy in ups:
        copy.wait()
    factor_up = jnp.concatenate(
        [
            jnp.concatenate([up_got[2 * quarter + part_of, s].astype(F32) for quarter in range(NY)], axis=1)
            for s in range(prompts)
            for part_of in range(2)
        ],
        axis=0,
    ).astype(BF16)
    for copy in lows:
        copy.wait()
    total = low_send_buf[0]
    for spot in range(7):
        total = total + low_got[spot]
    spread = jnp.concatenate([jnp.where(in_prompt(s, starts), total, 0.0) for s in range(prompts)], axis=0).T
    high = spread.astype(BF16)
    rest = (spread - high.astype(F32)).astype(BF16)
    delta = jnp.dot(high, factor_up, preferred_element_type=F32) + jnp.dot(
        rest, factor_up, preferred_element_type=F32
    )
    out_ref[...] = (acc[...] + delta).astype(BF16)

    for copy in xc:
        copy.wait_send()
    sent = gd.at[pl.ds(0, LINE - 1)]
    remote(sent, sent, d_send, d_send, z_peer(1)).wait_send()
    sent = gu.at[pl.ds(0, NZ - 1)]
    remote(sent, sent, u_send, u_send, z_peer(1)).wait_send()


def body(queries, key_rows, value_rows, lengths, adapter_ids, adapter_home, adapter_down, adapter_up, output_weight):
    rows, width = queries.shape
    rank = adapter_up.shape[1]
    prompts = lengths.shape[1]
    dma = pltpu.SemaphoreType.DMA
    hbm = pl.BlockSpec(memory_space=pltpu.HBM)
    block = pltpu.VMEM((rows, width), BF16)
    return pl.pallas_call(
        kernel,
        out_shape=jax.ShapeDtypeStruct((rows, width), BF16),
        in_specs=[hbm] * 9,
        out_specs=pl.BlockSpec(memory_space=pltpu.VMEM),
        scratch_shapes=[
            pltpu.SMEM(lengths.shape, jnp.int32),
            pltpu.SMEM(adapter_ids.shape, jnp.int32),
            pltpu.SMEM(adapter_home.shape, jnp.int32),
            block,
            block,
            block,
            pltpu.VMEM(output_weight.shape, BF16),
            pltpu.VMEM((LINE, rank, width), BF16),
            pltpu.VMEM((NZ, 2 * NY, rank // 2, width // NY), BF16),
            block,
            block,
            pltpu.VMEM((3, rows, width), BF16),
            pltpu.VMEM((2, rows, width), BF16),
            block,
            pltpu.VMEM((rows, width), F32),
            pltpu.VMEM((2 * NY, 8, 128), jnp.int32),
            pltpu.SMEM((2 * NY, 8, 128), jnp.int32),
            pltpu.VMEM((2 * NY - 1, prompts, rank // 2, width // NY), BF16),
            pltpu.VMEM((2 * NY, prompts, rank // 2, width // NY), BF16),
            pltpu.VMEM((2, rank, rows), F32),
            pltpu.VMEM((7, rank, rows), F32),
            dma((10,)),
            dma,
            dma,
            dma((NZ,)),
            dma((NZ,)),
            dma((2, NZ)),
            dma((NZ,)),
            dma((6,)),
            dma((6,)),
            dma((7,)),
            dma((7,)),
            dma((2,)),
            dma((7,)),
            dma((7,)),
            dma((7,)),
            dma((7,)),
            dma((7,)),
            dma((7,)),
        ],
        compiler_params=pltpu.CompilerParams(
            collective_id=0, has_side_effects=True, vmem_limit_bytes=VMEM_LIMIT
        ),
    )(
        *(
            pltpu.with_memory_space_constraint(operand, pltpu.HBM)
            for operand in (
                lengths,
                adapter_ids,
                adapter_home,
                queries,
                key_rows,
                value_rows,
                jnp.swapaxes(adapter_down, 1, 2),
                adapter_up,
                output_weight,
            )
        )
    )


VMEM_LIMIT = 40 * 1024 * 1024


def solution(mesh):
    return jax.shard_map(
        body,
        mesh=mesh,
        in_specs=(
            P("req", "tp"),
            P("req", "tp"),
            P("req", "tp"),
            P("req", None),
            P("req", None),
            P(),
            P("req", "tp", None),
            P("req", None, None),
            P("tp", None),
        ),
        out_specs=P("req", "tp"),
        check_vma=False,
    )
```

```python
import math

import jax
import jax.numpy as jnp
from jax import lax
from jax.experimental import pallas as pl
from jax.experimental.pallas import tpu as pltpu
from jax.sharding import PartitionSpec as P

HD = 128
NY, NZ, NX = 4, 16, 4
LINE = NY * NZ
MESH = pl.DeviceIdType.MESH
F32 = jnp.float32
BF16 = jnp.bfloat16

DOWN_TREE = {0: (4, 2, 1), 2: (3,), 4: (8, 7, 6, 5)}
UP_TREE = {0: (4, 2, 1), 2: (3,), 4: (8, 7, 6, 5)}


def offsets_at(distance):
    return (distance,) if distance in (0, NZ // 2) else (NZ - distance, distance)


def kernel(
    len_h,
    ids_h,
    home_h,
    q_h,
    k_h,
    v_h,
    dn_h,
    up_h,
    w_h,
    out_ref,
    len_s,
    ids_s,
    home_s,
    qv,
    kv,
    vv,
    wv,
    gd,
    gu,
    att,
    att_other,
    part,
    got,
    fwd_part,
    acc,
    note_all,
    note_s,
    up_send,
    up_got,
    low_send_buf,
    low_got,
    load_sem,
    d_send,
    u_send,
    zd_recv,
    zu_recv,
    y_recv,
    o_recv,
    x_send,
    x_recv,
    note_send,
    note_recv,
    att_sem,
    piece_send,
    piece_recv,
    up_sem_send,
    up_sem_recv,
    low_send,
    low_recv,
):
    req = lax.axis_index("req")
    x = lax.axis_index("tp")
    core = lax.rem(req, 2)
    z = lax.rem(lax.div(req, 2), NZ)
    y = lax.div(req, 2 * NZ)
    rows, width = qv.shape
    half = rows // 2
    prompts = ids_s.shape[1]
    rank = gd.shape[1]

    def place(y_at, z_at, core_at):
        return (y_at * NZ + z_at) * 2 + core_at

    def shifted(at, by, size):
        return lax.rem(at + by % size, size)

    def z_peer(by):
        return (place(y, shifted(z, by, NZ), core), x)

    def y_peer(by, other=0):
        return (place(shifted(y, by, NY), z, 1 - core if other else core), x)

    def x_peer(by, other=0):
        return (place(y, z, 1 - core if other else core), shifted(x, by, NX))

    partner = y_peer(0, 1)

    def line(y_by, offset):
        return shifted(y, y_by, NY) * NZ + shifted(z, offset, NZ)

    def remote(src, dst, send, recv, device):
        return pltpu.make_async_remote_copy(
            src_ref=src, dst_ref=dst, send_sem=send, recv_sem=recv, device_id=device, device_id_type=MESH
        )

    plane = [(by, other) for by in range(NY) for other in range(2) if (by, other) != (0, 0)]

    seat = 2 * y + core
    tile = width // NY

    def piece_of(by, other):
        first = pl.multiple_of((1 - core if other else core) * (rank // 2), rank // 2)
        column = pl.multiple_of(x * width + shifted(y, by, NY) * tile, tile)
        return up_h.at[0, pl.ds(first, rank // 2), pl.ds(column, tile)]

    loads = [
        pltpu.make_async_copy(dn_h.at[0], gd.at[line(0, 0)], load_sem.at[0]),
        pltpu.make_async_copy(piece_of(0, 0), gu.at[z, seat], load_sem.at[1]),
        pltpu.make_async_copy(len_h, len_s, load_sem.at[2]),
        pltpu.make_async_copy(ids_h, ids_s, load_sem.at[3]),
        pltpu.make_async_copy(home_h, home_s, load_sem.at[4]),
        pltpu.make_async_copy(q_h, qv, load_sem.at[5]),
        pltpu.make_async_copy(k_h, kv, load_sem.at[6]),
        pltpu.make_async_copy(v_h, vv, load_sem.at[7]),
        pltpu.make_async_copy(w_h, wv, load_sem.at[8]),
    ]
    for load in loads:
        load.start()
    barrier = pltpu.get_barrier_semaphore()
    peers = [z_peer(b) for b in (4, -4, 3, -3, 2, -2, 1, -1)] + [y_peer(b, o) for b, o in plane]
    peers += [x_peer(b, o) for b in range(1, NX) for o in range(2)]
    for peer in peers:
        pl.semaphore_signal(barrier, inc=1, device_id=peer, device_id_type=MESH)
    loads[0].wait()
    pl.semaphore_wait(barrier, len(peers))

    def z_bank(p, offset):
        return gu.at[shifted(z, offset, NZ)] if p else gd.at[line(0, offset)]

    z_recv = (zd_recv, zu_recv)
    z_send_sem = (d_send, u_send)

    def z_pass(p, offset):
        distance = min(offset, NZ - offset)
        for target in (UP_TREE if p else DOWN_TREE).get(distance, ()):
            for sign in (1, -1):
                if target == NZ // 2 and sign < 0:
                    continue
                if distance and (offset > NZ // 2) != (sign > 0):
                    continue
                by = sign * (target - distance)
                bank = z_bank(p, offset)
                remote(bank, bank, z_send_sem[p], z_recv[p].at[(offset - by) % NZ], z_peer(by)).start()

    def y_pass(offset):
        bank = gd.at[line(0, offset)]
        remote(bank, bank, d_send, o_recv.at[offset], y_peer(2)).start()
        for way, by in ((0, 1), (1, -1)):
            remote(bank, bank, d_send, y_recv.at[way, offset], y_peer(by)).start()

    def z_take(p, *distances):
        for distance in distances:
            for offset in offsets_at(distance):
                bank = z_bank(p, offset)
                remote(bank, bank, z_send_sem[p], z_recv[p].at[offset], z_peer(1)).wait_recv()
                z_pass(p, offset)
                if p == 0:
                    y_pass(offset)

    def y_take(*distances):
        for distance in distances:
            for offset in offsets_at(distance):
                for way, by in ((0, 1), (1, -1)):
                    bank = gd.at[line(-by, offset)]
                    remote(bank, bank, d_send, y_recv.at[way, offset], y_peer(by)).wait_recv()

    def o_take(*distances):
        for distance in distances:
            for offset in offsets_at(distance):
                bank = gd.at[line(2, offset)]
                remote(bank, bank, d_send, o_recv.at[offset], y_peer(1)).wait_recv()

    z_pass(0, 0)
    y_pass(0)
    pieces = [
        remote(piece_of(by, other), gu.at[z, seat], piece_send.at[i], piece_recv.at[i], y_peer(by, other))
        for i, (by, other) in enumerate(plane)
    ]
    for copy in pieces:
        copy.start()

    for load in loads[2:5]:
        load.wait()
    starts = []
    edge = jnp.int32(0)
    for s in range(prompts - 1):
        edge = edge + len_s[0, s]
        starts.append(edge)
    homes = [home_s[ids_s[0, s]] for s in range(prompts)]
    lane = lax.broadcasted_iota(jnp.int32, (8, 128), 1)
    note = jnp.zeros((8, 128), jnp.int32)
    for i, value in enumerate(homes + starts):
        note = jnp.where(lane == i, value, note)
    note_all[0] = note
    notes = []
    for i, (by, other) in enumerate(plane):
        spot = 2 * ((NY - by) % NY) + other
        notes.append(remote(note_all.at[0], note_all.at[spot], note_send.at[i], note_recv.at[i], y_peer(by, other)))
    for copy in notes:
        copy.start()

    def allowed_of(first, count, keys):
        row = lax.broadcasted_iota(jnp.int32, (count, keys), 0) + first
        key = lax.broadcasted_iota(jnp.int32, (count, keys), 1)
        begin = jnp.zeros((count, keys), jnp.int32)
        for start in starts:
            begin = jnp.where(row >= start, start, begin)
        return (key <= row) & (key >= begin)

    def attend(first, keys):
        allowed = allowed_of(first, half, keys)
        for head in range(width // HD):
            cols = slice(head * HD, (head + 1) * HD)
            scores = lax.dot_general(
                qv[first : first + half, cols],
                kv[:keys, cols],
                (((1,), (1,)), ((), ())),
                preferred_element_type=F32,
            ) * (1.0 / math.sqrt(HD))
            masked = jnp.where(allowed, scores, -1e30)
            highest = jnp.max(masked, axis=1, keepdims=True)
            exponent = jnp.exp(masked - highest)
            weights = (exponent * (1.0 / jnp.sum(exponent, axis=1, keepdims=True))).astype(BF16)
            mixed = jnp.dot(weights, vv[:keys, cols], preferred_element_type=F32)
            att[first : first + half, cols] = mixed.astype(BF16)

    def project(first, count, by):
        cols = pl.ds(pl.multiple_of(shifted(x, by, NX) * width, width), width)
        return jnp.dot(att[first : first + count, :], wv[:, cols], preferred_element_type=F32)

    top, low = slice(0, half), slice(half, rows)

    def x_copy(slot, src, dst, by):
        return remote(src, dst, x_send.at[slot], x_recv.at[slot], x_peer(by))

    xc = (
        x_copy(0, part.at[0, top], fwd_part.at[top], 1),
        x_copy(1, part.at[0, low], fwd_part.at[low], -1),
        x_copy(2, part.at[1, top], got.at[0, top], 1),
        x_copy(3, part.at[1, low], got.at[0, low], 1),
        x_copy(4, part.at[2, top], got.at[1, top], -1),
        x_copy(5, part.at[2, low], got.at[1, low], -1),
    )

    for load in loads[5:8]:
        load.wait()
    attend(0, half)
    loads[8].wait()
    part[0, top] = project(0, half, 2).astype(BF16)
    xc[0].start()
    loads[1].wait()
    for copy in pieces:
        copy.wait()
    z_pass(1, 0)
    z_take(0, 1, 2)
    attend(half, rows)
    part[0, low] = project(half, half, 2).astype(BF16)
    xc[1].start()
    att_copy = remote(att, att_other, att_sem.at[0], att_sem.at[1], partner)
    att_copy.start()
    part[1, low] = project(half, half, 1).astype(BF16)
    xc[3].start()
    part[2, top] = project(0, half, -1).astype(BF16)
    xc[4].start()
    z_take(0, 4, 3)
    y_take(0, 1, 2)
    part[1, top] = project(0, half, 1).astype(BF16)
    part[2, low] = project(half, half, -1).astype(BF16)
    acc[...] = project(0, rows, 0)
    for copy in notes:
        copy.wait()
    notes_local = pltpu.make_async_copy(note_all, note_s, load_sem.at[9])
    notes_local.start()
    xc[0].wait_recv()
    part[1, top] = (part[1, top].astype(F32) + fwd_part[top].astype(F32)).astype(BF16)
    xc[2].start()
    xc[1].wait_recv()
    part[2, low] = (part[2, low].astype(F32) + fwd_part[low].astype(F32)).astype(BF16)
    xc[5].start()
    z_take(1, 1, 2, 4)
    z_take(0, 5, 6)
    y_take(3, 4)
    z_take(0, 8, 7)
    z_take(1, 3)
    notes_local.wait()
    y_take(5, 6, 8, 7)
    z_take(1, 5, 6, 8, 7)

    def pick_up(spot, s):
        home = note_s[spot, 0, s]
        return gu[lax.rem(lax.div(home, 2), NZ), 2 * lax.div(home, 2 * NZ) + lax.rem(home, 2)]

    ups = []
    for i, (by, other) in enumerate(plane):
        for s in range(prompts):
            up_send[i, s] = pick_up(2 * by + other, s)
        ups.append(remote(up_send.at[i], up_got.at[seat], up_sem_send.at[i], up_sem_recv.at[i], y_peer(by, other)))
        ups[-1].start()
    for s in range(prompts):
        up_got[seat, s] = pick_up(0, s)
    for c in (2, 3, 4, 5):
        xc[c].wait_recv()
    acc[...] += got[0].astype(F32) + got[1].astype(F32)
    att_copy.wait()
    o_take(0, 1, 2, 3, 4, 5, 6, 8, 7)

    token = lax.broadcasted_iota(jnp.int32, (rank, rows), 1)

    def in_prompt(s, begins):
        inside = token >= begins[s - 1] if s else token >= 0
        return inside & (token < begins[s]) if s < prompts - 1 else inside

    def low_rank(spot, rows_ref):
        factors = []
        for s in range(prompts):
            home = note_s[spot, 0, s]
            factors.append(jnp.where(lax.rem(home, 2) == core, gd[lax.div(home, 2)], 0).astype(BF16))
        begins = [note_s[spot, 0, prompts + s] for s in range(prompts - 1)]
        every = lax.dot_general(
            jnp.concatenate(factors, axis=0), rows_ref[...], (((1,), (1,)), ((), ())), preferred_element_type=F32
        )
        total = jnp.zeros((rank, rows), F32)
        for s in range(prompts):
            total = total + jnp.where(in_prompt(s, begins), every[s * rank : (s + 1) * rank, :], 0.0)
        return total

    low_send_buf[0] = low_rank(0, att)
    lows = []

    def low_copy(which, spot, device):
        copy = remote(low_send_buf.at[which], low_got.at[spot], low_send.at[spot], low_recv.at[spot], device)
        copy.start()
        lows.append(copy)

    for by in (2, 1, 3):
        low_copy(0, by - 1, x_peer(by))
    low_send_buf[1] = low_rank(1, att_other)
    for by in (2, 1, 3, 0):
        low_copy(1, by + 3, x_peer(by, 1))

    for copy in ups:
        copy.wait()
    factor_up = jnp.concatenate(
        [
            jnp.concatenate([up_got[2 * quarter + part_of, s].astype(F32) for quarter in range(NY)], axis=1)
            for s in range(prompts)
            for part_of in range(2)
        ],
        axis=0,
    ).astype(BF16)
    for copy in lows:
        copy.wait()
    total = low_send_buf[0]
    for spot in range(7):
        total = total + low_got[spot]
    spread = jnp.concatenate([jnp.where(in_prompt(s, starts), total, 0.0) for s in range(prompts)], axis=0).T
    high = spread.astype(BF16)
    rest = (spread - high.astype(F32)).astype(BF16)
    delta = jnp.dot(high, factor_up, preferred_element_type=F32) + jnp.dot(
        rest, factor_up, preferred_element_type=F32
    )
    out_ref[...] = (acc[...] + delta).astype(BF16)

    for copy in xc:
        copy.wait_send()
    sent = gd.at[pl.ds(0, LINE - 1)]
    remote(sent, sent, d_send, d_send, z_peer(1)).wait_send()
    sent = gu.at[pl.ds(0, NZ - 1)]
    remote(sent, sent, u_send, u_send, z_peer(1)).wait_send()


def body(queries, key_rows, value_rows, lengths, adapter_ids, adapter_home, adapter_down, adapter_up, output_weight):
    rows, width = queries.shape
    rank = adapter_up.shape[1]
    prompts = lengths.shape[1]
    dma = pltpu.SemaphoreType.DMA
    hbm = pl.BlockSpec(memory_space=pltpu.HBM)
    block = pltpu.VMEM((rows, width), BF16)
    return pl.pallas_call(
        kernel,
        out_shape=jax.ShapeDtypeStruct((rows, width), BF16),
        in_specs=[hbm] * 9,
        out_specs=pl.BlockSpec(memory_space=pltpu.VMEM),
        scratch_shapes=[
            pltpu.SMEM(lengths.shape, jnp.int32),
            pltpu.SMEM(adapter_ids.shape, jnp.int32),
            pltpu.SMEM(adapter_home.shape, jnp.int32),
            block,
            block,
            block,
            pltpu.VMEM(output_weight.shape, BF16),
            pltpu.VMEM((LINE, rank, width), BF16),
            pltpu.VMEM((NZ, 2 * NY, rank // 2, width // NY), BF16),
            block,
            block,
            pltpu.VMEM((3, rows, width), BF16),
            pltpu.VMEM((2, rows, width), BF16),
            block,
            pltpu.VMEM((rows, width), F32),
            pltpu.VMEM((2 * NY, 8, 128), jnp.int32),
            pltpu.SMEM((2 * NY, 8, 128), jnp.int32),
            pltpu.VMEM((2 * NY - 1, prompts, rank // 2, width // NY), BF16),
            pltpu.VMEM((2 * NY, prompts, rank // 2, width // NY), BF16),
            pltpu.VMEM((2, rank, rows), F32),
            pltpu.VMEM((7, rank, rows), F32),
            dma((10,)),
            dma,
            dma,
            dma((NZ,)),
            dma((NZ,)),
            dma((2, NZ)),
            dma((NZ,)),
            dma((6,)),
            dma((6,)),
            dma((7,)),
            dma((7,)),
            dma((2,)),
            dma((7,)),
            dma((7,)),
            dma((7,)),
            dma((7,)),
            dma((7,)),
            dma((7,)),
        ],
        compiler_params=pltpu.CompilerParams(
            collective_id=0, has_side_effects=True, vmem_limit_bytes=VMEM_LIMIT
        ),
    )(
        *(
            pltpu.with_memory_space_constraint(operand, pltpu.HBM)
            for operand in (
                lengths,
                adapter_ids,
                adapter_home,
                queries,
                key_rows,
                value_rows,
                jnp.swapaxes(adapter_down, 1, 2),
                adapter_up,
                output_weight,
            )
        )
    )


VMEM_LIMIT = 40 * 1024 * 1024


def solution(mesh):
    return jax.shard_map(
        body,
        mesh=mesh,
        in_specs=(
            P("req", "tp"),
            P("req", "tp"),
            P("req", "tp"),
            P("req", None),
            P("req", None),
            P(),
            P("req", "tp", None),
            P("req", None, None),
            P("tp", None),
        ),
        out_specs=P("req", "tp"),
        check_vma=False,
    )
```

```python
import math

import jax
import jax.numpy as jnp
from jax import lax
from jax.experimental import pallas as pl
from jax.experimental.pallas import tpu as pltpu
from jax.sharding import PartitionSpec as P

HD = 128
NY, NZ, NX = 4, 16, 4
LINE = NY * NZ
MESH = pl.DeviceIdType.MESH
F32 = jnp.float32
BF16 = jnp.bfloat16

DOWN_TREE = {0: (4, 2, 1), 2: (3,), 4: (8, 7, 6, 5)}
UP_TREE = {0: (4, 2, 1), 2: (3,), 4: (8, 7, 6, 5)}


def offsets_at(distance):
    return (distance,) if distance in (0, NZ // 2) else (NZ - distance, distance)


def kernel(
    len_h,
    ids_h,
    home_h,
    q_h,
    k_h,
    v_h,
    dn_h,
    up_h,
    w_h,
    out_ref,
    len_s,
    ids_s,
    home_s,
    qv,
    kv,
    vv,
    wv,
    gd,
    gu,
    att,
    att_other,
    part,
    got,
    fwd_part,
    acc,
    note_all,
    note_s,
    up_send,
    up_got,
    low_send_buf,
    low_got,
    load_sem,
    d_send,
    u_send,
    zd_recv,
    zu_recv,
    y_recv,
    o_recv,
    x_send,
    x_recv,
    note_send,
    note_recv,
    att_sem,
    piece_send,
    piece_recv,
    up_sem_send,
    up_sem_recv,
    low_send,
    low_recv,
):
    req = lax.axis_index("req")
    x = lax.axis_index("tp")
    core = lax.rem(req, 2)
    z = lax.rem(lax.div(req, 2), NZ)
    y = lax.div(req, 2 * NZ)
    rows, width = qv.shape
    half = rows // 2
    prompts = ids_s.shape[1]
    rank = gd.shape[1]

    def place(y_at, z_at, core_at):
        return (y_at * NZ + z_at) * 2 + core_at

    def shifted(at, by, size):
        return lax.rem(at + by % size, size)

    def z_peer(by):
        return (place(y, shifted(z, by, NZ), core), x)

    def y_peer(by, other=0):
        return (place(shifted(y, by, NY), z, 1 - core if other else core), x)

    def x_peer(by, other=0):
        return (place(y, z, 1 - core if other else core), shifted(x, by, NX))

    partner = y_peer(0, 1)

    def line(y_by, offset):
        return shifted(y, y_by, NY) * NZ + shifted(z, offset, NZ)

    def remote(src, dst, send, recv, device):
        return pltpu.make_async_remote_copy(
            src_ref=src, dst_ref=dst, send_sem=send, recv_sem=recv, device_id=device, device_id_type=MESH
        )

    plane = [(by, other) for by in range(NY) for other in range(2) if (by, other) != (0, 0)]

    seat = 2 * y + core
    tile = width // NY

    def piece_of(by, other):
        first = pl.multiple_of((1 - core if other else core) * (rank // 2), rank // 2)
        column = pl.multiple_of(x * width + shifted(y, by, NY) * tile, tile)
        return up_h.at[0, pl.ds(first, rank // 2), pl.ds(column, tile)]

    loads = [
        pltpu.make_async_copy(dn_h.at[0], gd.at[line(0, 0)], load_sem.at[0]),
        pltpu.make_async_copy(piece_of(0, 0), gu.at[z, seat], load_sem.at[1]),
        pltpu.make_async_copy(len_h, len_s, load_sem.at[2]),
        pltpu.make_async_copy(ids_h, ids_s, load_sem.at[3]),
        pltpu.make_async_copy(home_h, home_s, load_sem.at[4]),
        pltpu.make_async_copy(q_h, qv, load_sem.at[5]),
        pltpu.make_async_copy(k_h, kv, load_sem.at[6]),
        pltpu.make_async_copy(v_h, vv, load_sem.at[7]),
        pltpu.make_async_copy(w_h, wv, load_sem.at[8]),
    ]
    for load in loads:
        load.start()
    barrier = pltpu.get_barrier_semaphore()
    peers = [z_peer(b) for b in (4, -4, 3, -3, 2, -2, 1, -1)] + [y_peer(b, o) for b, o in plane]
    peers += [x_peer(b, o) for b in range(1, NX) for o in range(2)]
    for peer in peers:
        pl.semaphore_signal(barrier, inc=1, device_id=peer, device_id_type=MESH)
    loads[0].wait()
    pl.semaphore_wait(barrier, len(peers))

    def z_bank(p, offset):
        return gu.at[shifted(z, offset, NZ)] if p else gd.at[line(0, offset)]

    z_recv = (zd_recv, zu_recv)
    z_send_sem = (d_send, u_send)

    def z_pass(p, offset):
        distance = min(offset, NZ - offset)
        for target in (UP_TREE if p else DOWN_TREE).get(distance, ()):
            for sign in (1, -1):
                if target == NZ // 2 and sign != (-1 if p else 1):
                    continue
                if distance and (offset > NZ // 2) != (sign > 0):
                    continue
                by = sign * (target - distance)
                bank = z_bank(p, offset)
                remote(bank, bank, z_send_sem[p], z_recv[p].at[(offset - by) % NZ], z_peer(by)).start()

    def y_pass(offset):
        bank = gd.at[line(0, offset)]
        remote(bank, bank, d_send, o_recv.at[offset], y_peer(2)).start()
        for way, by in ((0, 1), (1, -1)):
            remote(bank, bank, d_send, y_recv.at[way, offset], y_peer(by)).start()

    def z_take(p, *distances):
        for distance in distances:
            for offset in offsets_at(distance):
                bank = z_bank(p, offset)
                remote(bank, bank, z_send_sem[p], z_recv[p].at[offset], z_peer(1)).wait_recv()
                z_pass(p, offset)
                if p == 0:
                    y_pass(offset)

    def y_take(*distances):
        for distance in distances:
            for offset in offsets_at(distance):
                for way, by in ((0, 1), (1, -1)):
                    bank = gd.at[line(-by, offset)]
                    remote(bank, bank, d_send, y_recv.at[way, offset], y_peer(by)).wait_recv()

    def o_take(*distances):
        for distance in distances:
            for offset in offsets_at(distance):
                bank = gd.at[line(2, offset)]
                remote(bank, bank, d_send, o_recv.at[offset], y_peer(1)).wait_recv()

    z_pass(0, 0)
    pieces = [
        remote(piece_of(by, other), gu.at[z, seat], piece_send.at[i], piece_recv.at[i], y_peer(by, other))
        for i, (by, other) in enumerate(plane)
    ]
    for copy in pieces:
        copy.start()
    y_pass(0)

    for load in loads[2:5]:
        load.wait()
    starts = []
    edge = jnp.int32(0)
    for s in range(prompts - 1):
        edge = edge + len_s[0, s]
        starts.append(edge)
    homes = [home_s[ids_s[0, s]] for s in range(prompts)]
    lane = lax.broadcasted_iota(jnp.int32, (8, 128), 1)
    note = jnp.zeros((8, 128), jnp.int32)
    for i, value in enumerate(homes + starts):
        note = jnp.where(lane == i, value, note)
    note_all[0] = note
    notes = []
    for i, (by, other) in enumerate(plane):
        spot = 2 * ((NY - by) % NY) + other
        notes.append(remote(note_all.at[0], note_all.at[spot], note_send.at[i], note_recv.at[i], y_peer(by, other)))
    for copy in notes:
        copy.start()

    def allowed_of(first, count, keys):
        row = lax.broadcasted_iota(jnp.int32, (count, keys), 0) + first
        key = lax.broadcasted_iota(jnp.int32, (count, keys), 1)
        begin = jnp.zeros((count, keys), jnp.int32)
        for start in starts:
            begin = jnp.where(row >= start, start, begin)
        return (key <= row) & (key >= begin)

    def attend(first, keys):
        allowed = allowed_of(first, half, keys)
        for head in range(width // HD):
            cols = slice(head * HD, (head + 1) * HD)
            scores = lax.dot_general(
                qv[first : first + half, cols],
                kv[:keys, cols],
                (((1,), (1,)), ((), ())),
                preferred_element_type=F32,
            ) * (1.0 / math.sqrt(HD))
            masked = jnp.where(allowed, scores, -1e30)
            highest = jnp.max(masked, axis=1, keepdims=True)
            exponent = jnp.exp(masked - highest)
            weights = (exponent * (1.0 / jnp.sum(exponent, axis=1, keepdims=True))).astype(BF16)
            mixed = jnp.dot(weights, vv[:keys, cols], preferred_element_type=F32)
            att[first : first + half, cols] = mixed.astype(BF16)

    def project(first, count, by):
        cols = pl.ds(pl.multiple_of(shifted(x, by, NX) * width, width), width)
        return jnp.dot(att[first : first + count, :], wv[:, cols], preferred_element_type=F32)

    top, low = slice(0, half), slice(half, rows)

    def x_copy(slot, src, dst, by):
        return remote(src, dst, x_send.at[slot], x_recv.at[slot], x_peer(by))

    xc = (
        x_copy(0, part.at[0, top], fwd_part.at[top], 1),
        x_copy(1, part.at[0, low], fwd_part.at[low], -1),
        x_copy(2, part.at[1, top], got.at[0, top], 1),
        x_copy(3, part.at[1, low], got.at[0, low], 1),
        x_copy(4, part.at[2, top], got.at[1, top], -1),
        x_copy(5, part.at[2, low], got.at[1, low], -1),
    )

    for load in loads[5:8]:
        load.wait()
    attend(0, half)
    loads[8].wait()
    part[0, top] = project(0, half, 2).astype(BF16)
    xc[0].start()
    loads[1].wait()
    for copy in pieces:
        copy.wait()
    z_pass(1, 0)
    z_take(0, 1, 2)
    attend(half, rows)
    part[0, low] = project(half, half, 2).astype(BF16)
    xc[1].start()
    att_copy = remote(att, att_other, att_sem.at[0], att_sem.at[1], partner)
    att_copy.start()
    part[1, low] = project(half, half, 1).astype(BF16)
    xc[3].start()
    part[2, top] = project(0, half, -1).astype(BF16)
    xc[4].start()
    z_take(0, 4, 3)
    y_take(0, 1, 2)
    part[1, top] = project(0, half, 1).astype(BF16)
    part[2, low] = project(half, half, -1).astype(BF16)
    acc[...] = project(0, rows, 0)
    for copy in notes:
        copy.wait()
    notes_local = pltpu.make_async_copy(note_all, note_s, load_sem.at[9])
    notes_local.start()
    xc[0].wait_recv()
    part[1, top] = (part[1, top].astype(F32) + fwd_part[top].astype(F32)).astype(BF16)
    xc[2].start()
    xc[1].wait_recv()
    part[2, low] = (part[2, low].astype(F32) + fwd_part[low].astype(F32)).astype(BF16)
    xc[5].start()
    z_take(1, 1, 2, 4)
    z_take(0, 5, 6)
    y_take(3, 4)
    z_take(0, 8, 7)
    z_take(1, 3)
    notes_local.wait()
    y_take(5, 6, 8, 7)
    z_take(1, 5, 6, 8, 7)

    def pick_up(spot, s):
        home = note_s[spot, 0, s]
        return gu[lax.rem(lax.div(home, 2), NZ), 2 * lax.div(home, 2 * NZ) + lax.rem(home, 2)]

    ups = []
    for i, (by, other) in enumerate(plane):
        for s in range(prompts):
            up_send[i, s] = pick_up(2 * by + other, s)
        ups.append(remote(up_send.at[i], up_got.at[seat], up_sem_send.at[i], up_sem_recv.at[i], y_peer(by, other)))
        ups[-1].start()
    for s in range(prompts):
        up_got[seat, s] = pick_up(0, s)
    att_copy.wait()
    o_take(0, 1, 2, 3, 4, 5, 6, 8, 7)

    token = lax.broadcasted_iota(jnp.int32, (rank, rows), 1)

    def in_prompt(s, begins):
        inside = token >= begins[s - 1] if s else token >= 0
        return inside & (token < begins[s]) if s < prompts - 1 else inside

    def low_rank(spot, rows_ref):
        factors = []
        for s in range(prompts):
            home = note_s[spot, 0, s]
            factors.append(jnp.where(lax.rem(home, 2) == core, gd[lax.div(home, 2)], 0).astype(BF16))
        begins = [note_s[spot, 0, prompts + s] for s in range(prompts - 1)]
        every = lax.dot_general(
            jnp.concatenate(factors, axis=0), rows_ref[...], (((1,), (1,)), ((), ())), preferred_element_type=F32
        )
        total = jnp.zeros((rank, rows), F32)
        for s in range(prompts):
            total = total + jnp.where(in_prompt(s, begins), every[s * rank : (s + 1) * rank, :], 0.0)
        return total

    low_send_buf[0] = low_rank(0, att)
    lows = []

    def low_copy(which, spot, device):
        copy = remote(low_send_buf.at[which], low_got.at[spot], low_send.at[spot], low_recv.at[spot], device)
        copy.start()
        lows.append(copy)

    for by in (2, 1, 3):
        low_copy(0, by - 1, x_peer(by))
    low_send_buf[1] = low_rank(1, att_other)
    for by in (2, 1, 3, 0):
        low_copy(1, by + 3, x_peer(by, 1))

    for c in (2, 3, 4, 5):
        xc[c].wait_recv()
    acc[...] += got[0].astype(F32) + got[1].astype(F32)
    for copy in ups:
        copy.wait()
    factor_up = jnp.concatenate(
        [
            jnp.concatenate([up_got[2 * quarter + part_of, s].astype(F32) for quarter in range(NY)], axis=1)
            for s in range(prompts)
            for part_of in range(2)
        ],
        axis=0,
    ).astype(BF16)
    for copy in lows:
        copy.wait()
    total = low_send_buf[0]
    for spot in range(7):
        total = total + low_got[spot]
    spread = jnp.concatenate([jnp.where(in_prompt(s, starts), total, 0.0) for s in range(prompts)], axis=0).T
    high = spread.astype(BF16)
    rest = (spread - high.astype(F32)).astype(BF16)
    delta = jnp.dot(high, factor_up, preferred_element_type=F32) + jnp.dot(
        rest, factor_up, preferred_element_type=F32
    )
    out_ref[...] = (acc[...] + delta).astype(BF16)

    for copy in xc:
        copy.wait_send()
    sent = gd.at[pl.ds(0, LINE - 1)]
    remote(sent, sent, d_send, d_send, z_peer(1)).wait_send()
    sent = gu.at[pl.ds(0, NZ - 1)]
    remote(sent, sent, u_send, u_send, z_peer(1)).wait_send()


def body(queries, key_rows, value_rows, lengths, adapter_ids, adapter_home, adapter_down, adapter_up, output_weight):
    rows, width = queries.shape
    rank = adapter_up.shape[1]
    prompts = lengths.shape[1]
    dma = pltpu.SemaphoreType.DMA
    hbm = pl.BlockSpec(memory_space=pltpu.HBM)
    block = pltpu.VMEM((rows, width), BF16)
    return pl.pallas_call(
        kernel,
        out_shape=jax.ShapeDtypeStruct((rows, width), BF16),
        in_specs=[hbm] * 9,
        out_specs=pl.BlockSpec(memory_space=pltpu.VMEM),
        scratch_shapes=[
            pltpu.SMEM(lengths.shape, jnp.int32),
            pltpu.SMEM(adapter_ids.shape, jnp.int32),
            pltpu.SMEM(adapter_home.shape, jnp.int32),
            block,
            block,
            block,
            pltpu.VMEM(output_weight.shape, BF16),
            pltpu.VMEM((LINE, rank, width), BF16),
            pltpu.VMEM((NZ, 2 * NY, rank // 2, width // NY), BF16),
            block,
            block,
            pltpu.VMEM((3, rows, width), BF16),
            pltpu.VMEM((2, rows, width), BF16),
            block,
            pltpu.VMEM((rows, width), F32),
            pltpu.VMEM((2 * NY, 8, 128), jnp.int32),
            pltpu.SMEM((2 * NY, 8, 128), jnp.int32),
            pltpu.VMEM((2 * NY - 1, prompts, rank // 2, width // NY), BF16),
            pltpu.VMEM((2 * NY, prompts, rank // 2, width // NY), BF16),
            pltpu.VMEM((2, rank, rows), F32),
            pltpu.VMEM((7, rank, rows), F32),
            dma((10,)),
            dma,
            dma,
            dma((NZ,)),
            dma((NZ,)),
            dma((2, NZ)),
            dma((NZ,)),
            dma((6,)),
            dma((6,)),
            dma((7,)),
            dma((7,)),
            dma((2,)),
            dma((7,)),
            dma((7,)),
            dma((7,)),
            dma((7,)),
            dma((7,)),
            dma((7,)),
        ],
        compiler_params=pltpu.CompilerParams(
            collective_id=0, has_side_effects=True, vmem_limit_bytes=VMEM_LIMIT
        ),
    )(
        *(
            pltpu.with_memory_space_constraint(operand, pltpu.HBM)
            for operand in (
                lengths,
                adapter_ids,
                adapter_home,
                queries,
                key_rows,
                value_rows,
                jnp.swapaxes(adapter_down, 1, 2),
                adapter_up,
                output_weight,
            )
        )
    )


VMEM_LIMIT = 40 * 1024 * 1024


def solution(mesh):
    return jax.shard_map(
        body,
        mesh=mesh,
        in_specs=(
            P("req", "tp"),
            P("req", "tp"),
            P("req", "tp"),
            P("req", None),
            P("req", None),
            P(),
            P("req", "tp", None),
            P("req", None, None),
            P("tp", None),
        ),
        out_specs=P("req", "tp"),
        check_vma=False,
    )
```

```python
import math

import jax
import jax.numpy as jnp
from jax import lax
from jax.experimental import pallas as pl
from jax.experimental.pallas import tpu as pltpu
from jax.sharding import PartitionSpec as P

HD = 128
NY, NZ, NX = 4, 16, 4
LINE = NY * NZ
MESH = pl.DeviceIdType.MESH
F32 = jnp.float32
BF16 = jnp.bfloat16

DOWN_TREE = {0: (4, 2, 1), 2: (3,), 4: (8, 7, 6, 5)}
UP_TREE = {0: (4, 2, 1), 2: (3,), 4: (8, 7, 6, 5)}


def offsets_at(distance):
    return (distance,) if distance in (0, NZ // 2) else (NZ - distance, distance)


def kernel(
    len_h,
    ids_h,
    home_h,
    q_h,
    k_h,
    v_h,
    dn_h,
    up_h,
    w_h,
    out_ref,
    len_s,
    ids_s,
    home_s,
    qv,
    kv,
    vv,
    wv,
    gd,
    gu,
    att,
    att_other,
    part,
    got,
    fwd_part,
    acc,
    note_all,
    note_s,
    up_send,
    up_got,
    low_send_buf,
    low_got,
    load_sem,
    d_send,
    u_send,
    zd_recv,
    zu_recv,
    y_recv,
    o_recv,
    x_send,
    x_recv,
    note_send,
    note_recv,
    att_sem,
    piece_send,
    piece_recv,
    up_sem_send,
    up_sem_recv,
    low_send,
    low_recv,
):
    req = lax.axis_index("req")
    x = lax.axis_index("tp")
    core = lax.rem(req, 2)
    z = lax.rem(lax.div(req, 2), NZ)
    y = lax.div(req, 2 * NZ)
    rows, width = qv.shape
    half = rows // 2
    prompts = ids_s.shape[1]
    rank = gd.shape[1]

    def place(y_at, z_at, core_at):
        return (y_at * NZ + z_at) * 2 + core_at

    def shifted(at, by, size):
        return lax.rem(at + by % size, size)

    def z_peer(by):
        return (place(y, shifted(z, by, NZ), core), x)

    def y_peer(by, other=0):
        return (place(shifted(y, by, NY), z, 1 - core if other else core), x)

    def x_peer(by, other=0):
        return (place(y, z, 1 - core if other else core), shifted(x, by, NX))

    partner = y_peer(0, 1)

    def line(y_by, offset):
        return shifted(y, y_by, NY) * NZ + shifted(z, offset, NZ)

    def remote(src, dst, send, recv, device):
        return pltpu.make_async_remote_copy(
            src_ref=src, dst_ref=dst, send_sem=send, recv_sem=recv, device_id=device, device_id_type=MESH
        )

    plane = [(by, other) for by in range(NY) for other in range(2) if (by, other) != (0, 0)]

    seat = 2 * y + core
    tile = width // NY

    def piece_of(by, other):
        first = pl.multiple_of((1 - core if other else core) * (rank // 2), rank // 2)
        column = pl.multiple_of(x * width + shifted(y, by, NY) * tile, tile)
        return up_h.at[0, pl.ds(first, rank // 2), pl.ds(column, tile)]

    loads = [
        pltpu.make_async_copy(dn_h.at[0], gd.at[line(0, 0)], load_sem.at[0]),
        pltpu.make_async_copy(piece_of(0, 0), gu.at[z, seat], load_sem.at[1]),
        pltpu.make_async_copy(len_h, len_s, load_sem.at[2]),
        pltpu.make_async_copy(ids_h, ids_s, load_sem.at[3]),
        pltpu.make_async_copy(home_h, home_s, load_sem.at[4]),
        pltpu.make_async_copy(q_h, qv, load_sem.at[5]),
        pltpu.make_async_copy(k_h, kv, load_sem.at[6]),
        pltpu.make_async_copy(v_h, vv, load_sem.at[7]),
        pltpu.make_async_copy(w_h, wv, load_sem.at[8]),
    ]
    for load in loads:
        load.start()
    barrier = pltpu.get_barrier_semaphore()
    peers = [z_peer(b) for b in (4, -4, 3, -3, 2, -2, 1, -1)] + [y_peer(b, o) for b, o in plane]
    peers += [x_peer(b, o) for b in range(1, NX) for o in range(2)]
    for peer in peers:
        pl.semaphore_signal(barrier, inc=1, device_id=peer, device_id_type=MESH)
    loads[0].wait()
    pl.semaphore_wait(barrier, len(peers))

    def z_bank(p, offset):
        return gu.at[shifted(z, offset, NZ)] if p else gd.at[line(0, offset)]

    z_recv = (zd_recv, zu_recv)
    z_send_sem = (d_send, u_send)

    def z_pass(p, offset):
        distance = min(offset, NZ - offset)
        for target in (UP_TREE if p else DOWN_TREE).get(distance, ()):
            for sign in (1, -1):
                if target == NZ // 2 and sign != (-1 if p else 1):
                    continue
                if distance and (offset > NZ // 2) != (sign > 0):
                    continue
                by = sign * (target - distance)
                bank = z_bank(p, offset)
                remote(bank, bank, z_send_sem[p], z_recv[p].at[(offset - by) % NZ], z_peer(by)).start()

    def y_pass(offset):
        bank = gd.at[line(0, offset)]
        remote(bank, bank, d_send, o_recv.at[offset], y_peer(2)).start()
        for way, by in ((0, 1), (1, -1)):
            remote(bank, bank, d_send, y_recv.at[way, offset], y_peer(by)).start()

    def z_take(p, *distances):
        for distance in distances:
            for offset in offsets_at(distance):
                bank = z_bank(p, offset)
                remote(bank, bank, z_send_sem[p], z_recv[p].at[offset], z_peer(1)).wait_recv()
                z_pass(p, offset)
                if p == 0:
                    y_pass(offset)

    def y_take(*distances):
        for distance in distances:
            for offset in offsets_at(distance):
                for way, by in ((0, 1), (1, -1)):
                    bank = gd.at[line(-by, offset)]
                    remote(bank, bank, d_send, y_recv.at[way, offset], y_peer(by)).wait_recv()

    def o_take(*distances):
        for distance in distances:
            for offset in offsets_at(distance):
                bank = gd.at[line(2, offset)]
                remote(bank, bank, d_send, o_recv.at[offset], y_peer(1)).wait_recv()

    z_pass(0, 0)
    pieces = [
        remote(piece_of(by, other), gu.at[z, seat], piece_send.at[i], piece_recv.at[i], y_peer(by, other))
        for i, (by, other) in enumerate(plane)
    ]
    for copy in pieces:
        copy.start()
    y_pass(0)

    for load in loads[2:5]:
        load.wait()
    starts = []
    edge = jnp.int32(0)
    for s in range(prompts - 1):
        edge = edge + len_s[0, s]
        starts.append(edge)
    homes = [home_s[ids_s[0, s]] for s in range(prompts)]
    lane = lax.broadcasted_iota(jnp.int32, (8, 128), 1)
    note = jnp.zeros((8, 128), jnp.int32)
    for i, value in enumerate(homes + starts):
        note = jnp.where(lane == i, value, note)
    note_all[0] = note
    notes = []
    for i, (by, other) in enumerate(plane):
        spot = 2 * ((NY - by) % NY) + other
        notes.append(remote(note_all.at[0], note_all.at[spot], note_send.at[i], note_recv.at[i], y_peer(by, other)))
    for copy in notes:
        copy.start()

    def allowed_of(first, count, keys):
        row = lax.broadcasted_iota(jnp.int32, (count, keys), 0) + first
        key = lax.broadcasted_iota(jnp.int32, (count, keys), 1)
        begin = jnp.zeros((count, keys), jnp.int32)
        for start in starts:
            begin = jnp.where(row >= start, start, begin)
        return (key <= row) & (key >= begin)

    def attend(first, keys):
        allowed = allowed_of(first, half, keys)
        for head in range(width // HD):
            cols = slice(head * HD, (head + 1) * HD)
            scores = lax.dot_general(
                qv[first : first + half, cols],
                kv[:keys, cols],
                (((1,), (1,)), ((), ())),
                preferred_element_type=F32,
            ) * (1.0 / math.sqrt(HD))
            masked = jnp.where(allowed, scores, -1e30)
            highest = jnp.max(masked, axis=1, keepdims=True)
            exponent = jnp.exp(masked - highest)
            weights = (exponent * (1.0 / jnp.sum(exponent, axis=1, keepdims=True))).astype(BF16)
            mixed = jnp.dot(weights, vv[:keys, cols], preferred_element_type=F32)
            att[first : first + half, cols] = mixed.astype(BF16)

    def project(first, count, by):
        cols = pl.ds(pl.multiple_of(shifted(x, by, NX) * width, width), width)
        return jnp.dot(att[first : first + count, :], wv[:, cols], preferred_element_type=F32)

    top, low = slice(0, half), slice(half, rows)

    def x_copy(slot, src, dst, by):
        return remote(src, dst, x_send.at[slot], x_recv.at[slot], x_peer(by))

    xc = (
        x_copy(0, part.at[0, top], fwd_part.at[top], 1),
        x_copy(1, part.at[0, low], fwd_part.at[low], -1),
        x_copy(2, part.at[1, top], got.at[0, top], 1),
        x_copy(3, part.at[1, low], got.at[0, low], 1),
        x_copy(4, part.at[2, top], got.at[1, top], -1),
        x_copy(5, part.at[2, low], got.at[1, low], -1),
    )

    for load in loads[5:8]:
        load.wait()
    attend(0, half)
    loads[8].wait()
    part[0, top] = project(0, half, 2).astype(BF16)
    xc[0].start()
    loads[1].wait()
    for copy in pieces:
        copy.wait()
    z_pass(1, 0)
    z_take(0, 1, 2)
    attend(half, rows)
    part[0, low] = project(half, half, 2).astype(BF16)
    xc[1].start()
    att_copy = remote(att, att_other, att_sem.at[0], att_sem.at[1], partner)
    att_copy.start()
    part[1, low] = project(half, half, 1).astype(BF16)
    xc[3].start()
    part[2, top] = project(0, half, -1).astype(BF16)
    xc[4].start()
    z_take(0, 4, 3)
    y_take(0, 1, 2)
    part[1, top] = project(0, half, 1).astype(BF16)
    part[2, low] = project(half, half, -1).astype(BF16)
    acc[...] = project(0, rows, 0)
    for copy in notes:
        copy.wait()
    notes_local = pltpu.make_async_copy(note_all, note_s, load_sem.at[9])
    notes_local.start()
    xc[0].wait_recv()
    part[1, top] = (part[1, top].astype(F32) + fwd_part[top].astype(F32)).astype(BF16)
    xc[2].start()
    xc[1].wait_recv()
    part[2, low] = (part[2, low].astype(F32) + fwd_part[low].astype(F32)).astype(BF16)
    xc[5].start()
    z_take(1, 1, 2, 4)
    z_take(0, 5, 6)
    y_take(3, 4)
    z_take(0, 8, 7)
    z_take(1, 3)
    notes_local.wait()
    z_take(1, 5, 6, 8, 7)

    def pick_up(spot, s):
        home = note_s[spot, 0, s]
        return gu[lax.rem(lax.div(home, 2), NZ), 2 * lax.div(home, 2 * NZ) + lax.rem(home, 2)]

    ups = []
    for i, (by, other) in enumerate(plane):
        for s in range(prompts):
            up_send[i, s] = pick_up(2 * by + other, s)
        ups.append(remote(up_send.at[i], up_got.at[seat], up_sem_send.at[i], up_sem_recv.at[i], y_peer(by, other)))
        ups[-1].start()
    for s in range(prompts):
        up_got[seat, s] = pick_up(0, s)
    att_copy.wait()
    y_take(5, 6, 8, 7)
    o_take(0, 1, 2, 3, 4, 5, 6, 8, 7)

    token = lax.broadcasted_iota(jnp.int32, (rank, rows), 1)

    def in_prompt(s, begins):
        inside = token >= begins[s - 1] if s else token >= 0
        return inside & (token < begins[s]) if s < prompts - 1 else inside

    def low_rank(spot, rows_ref):
        factors = []
        for s in range(prompts):
            home = note_s[spot, 0, s]
            factors.append(jnp.where(lax.rem(home, 2) == core, gd[lax.div(home, 2)], 0).astype(BF16))
        begins = [note_s[spot, 0, prompts + s] for s in range(prompts - 1)]
        every = lax.dot_general(
            jnp.concatenate(factors, axis=0), rows_ref[...], (((1,), (1,)), ((), ())), preferred_element_type=F32
        )
        total = jnp.zeros((rank, rows), F32)
        for s in range(prompts):
            total = total + jnp.where(in_prompt(s, begins), every[s * rank : (s + 1) * rank, :], 0.0)
        return total

    low_send_buf[0] = low_rank(0, att)
    lows = []

    def low_copy(which, spot, device):
        copy = remote(low_send_buf.at[which], low_got.at[spot], low_send.at[spot], low_recv.at[spot], device)
        copy.start()
        lows.append(copy)

    for by in (2, 1, 3):
        low_copy(0, by - 1, x_peer(by))
    low_send_buf[1] = low_rank(1, att_other)
    for by in (2, 1, 3, 0):
        low_copy(1, by + 3, x_peer(by, 1))

    for c in (2, 3, 4, 5):
        xc[c].wait_recv()
    acc[...] += got[0].astype(F32) + got[1].astype(F32)
    for copy in ups:
        copy.wait()
    factor_up = jnp.concatenate(
        [
            jnp.concatenate([up_got[2 * quarter + part_of, s].astype(F32) for quarter in range(NY)], axis=1)
            for s in range(prompts)
            for part_of in range(2)
        ],
        axis=0,
    ).astype(BF16)
    for copy in lows:
        copy.wait()
    total = low_send_buf[0]
    for spot in range(7):
        total = total + low_got[spot]
    spread = jnp.concatenate([jnp.where(in_prompt(s, starts), total, 0.0) for s in range(prompts)], axis=0).T
    high = spread.astype(BF16)
    rest = (spread - high.astype(F32)).astype(BF16)
    delta = jnp.dot(high, factor_up, preferred_element_type=F32) + jnp.dot(
        rest, factor_up, preferred_element_type=F32
    )
    out_ref[...] = (acc[...] + delta).astype(BF16)

    for copy in xc:
        copy.wait_send()
    sent = gd.at[pl.ds(0, LINE - 1)]
    remote(sent, sent, d_send, d_send, z_peer(1)).wait_send()
    sent = gu.at[pl.ds(0, NZ - 1)]
    remote(sent, sent, u_send, u_send, z_peer(1)).wait_send()


def body(queries, key_rows, value_rows, lengths, adapter_ids, adapter_home, adapter_down, adapter_up, output_weight):
    rows, width = queries.shape
    rank = adapter_up.shape[1]
    prompts = lengths.shape[1]
    dma = pltpu.SemaphoreType.DMA
    hbm = pl.BlockSpec(memory_space=pltpu.HBM)
    block = pltpu.VMEM((rows, width), BF16)
    return pl.pallas_call(
        kernel,
        out_shape=jax.ShapeDtypeStruct((rows, width), BF16),
        in_specs=[hbm] * 9,
        out_specs=pl.BlockSpec(memory_space=pltpu.VMEM),
        scratch_shapes=[
            pltpu.SMEM(lengths.shape, jnp.int32),
            pltpu.SMEM(adapter_ids.shape, jnp.int32),
            pltpu.SMEM(adapter_home.shape, jnp.int32),
            block,
            block,
            block,
            pltpu.VMEM(output_weight.shape, BF16),
            pltpu.VMEM((LINE, rank, width), BF16),
            pltpu.VMEM((NZ, 2 * NY, rank // 2, width // NY), BF16),
            block,
            block,
            pltpu.VMEM((3, rows, width), BF16),
            pltpu.VMEM((2, rows, width), BF16),
            block,
            pltpu.VMEM((rows, width), F32),
            pltpu.VMEM((2 * NY, 8, 128), jnp.int32),
            pltpu.SMEM((2 * NY, 8, 128), jnp.int32),
            pltpu.VMEM((2 * NY - 1, prompts, rank // 2, width // NY), BF16),
            pltpu.VMEM((2 * NY, prompts, rank // 2, width // NY), BF16),
            pltpu.VMEM((2, rank, rows), F32),
            pltpu.VMEM((7, rank, rows), F32),
            dma((10,)),
            dma,
            dma,
            dma((NZ,)),
            dma((NZ,)),
            dma((2, NZ)),
            dma((NZ,)),
            dma((6,)),
            dma((6,)),
            dma((7,)),
            dma((7,)),
            dma((2,)),
            dma((7,)),
            dma((7,)),
            dma((7,)),
            dma((7,)),
            dma((7,)),
            dma((7,)),
        ],
        compiler_params=pltpu.CompilerParams(
            collective_id=0, has_side_effects=True, vmem_limit_bytes=VMEM_LIMIT
        ),
    )(
        *(
            pltpu.with_memory_space_constraint(operand, pltpu.HBM)
            for operand in (
                lengths,
                adapter_ids,
                adapter_home,
                queries,
                key_rows,
                value_rows,
                jnp.swapaxes(adapter_down, 1, 2),
                adapter_up,
                output_weight,
            )
        )
    )


VMEM_LIMIT = 40 * 1024 * 1024


def solution(mesh):
    return jax.shard_map(
        body,
        mesh=mesh,
        in_specs=(
            P("req", "tp"),
            P("req", "tp"),
            P("req", "tp"),
            P("req", None),
            P("req", None),
            P(),
            P("req", "tp", None),
            P("req", None, None),
            P("tp", None),
        ),
        out_specs=P("req", "tp"),
        check_vma=False,
    )
```
